128 devices in a mesh: dp: 64 (over z, y, x), ctx: 2 (over core).
Axes of the slice: x: 4, y: 4, z: 4, core: 2. Of those that a mesh axis runs over, the one named last changes fastest.
Arguments:
- tokens: bfloat16 [64, 512, 4096], P('dp', 'ctx'), may hold values from -16 to 16
- values: bfloat16 [64, 512, 8192], P('dp', 'ctx'), may hold values from -6 to 6
- log_decay: float32 [64, 512, 128], P('dp', 'ctx'), may hold values from -1 to 0, as said below
- out_grad: bfloat16 [64, 512, 8192], P('dp', 'ctx'), may hold values from -6 to 6
- proj_weight: bfloat16 [4096, 384], P('dp'), may hold values from -0.09375 to 0.09375
- dt_bias: float32 [128], replicated, may hold values from -4 to -2
- skip: float32 [128], replicated, may hold values from 0.5 to 1.5
- gain: float32 [8192], replicated, may hold values from 0.5 to 1.5
Outputs:
- mixed: bfloat16 [64, 512, 8192], P('dp', 'ctx')
- grad_tokens: bfloat16 [64, 512, 4096], P('dp', 'ctx')
- grad_values: bfloat16 [64, 512, 8192], P('dp', 'ctx')
- grad_log_decay: float32 [64, 512, 128], P('dp', 'ctx')
- grad_weight: float32 [4096, 384], P('dp')
The draws below stay inside these ranges and needn't reach their ends.
Inputs may be any that keep to these rules, and one draw needn't show every extreme that they name: log_decay is negative everywhere.
All inputs are finite; a program needn't handle non-finite values.
Results may differ from the reference program's by a relative error of at most 0.013.
Values may be sent and summed in bfloat16 or wider, within the bound.
No kernel may reach another device: no remote copies, remote signals or barrier semaphores. Data moves between devices by JAX's collectives and lax.ppermute only.
A program may use at most 256 MiB of HBM per device.

```python
import math
import jax
import jax.numpy as jnp
from jax import lax

D = 4096
SPACE_HEADS = 128
TOK_DEV = 256
ROLLOUT_BATCH = 64
SEQUENCE_LENGTH = 512
INNER = 8192
PROJ = 384


def draw_log_decay(key, part):
    random_subkeys = jax.random.split(key, 7)
    fast_share = 0.5
    fast_pick = jax.random.uniform(random_subkeys[0], (ROLLOUT_BATCH, 1, SPACE_HEADS)) < fast_share
    fast_rate = jnp.exp(jax.random.uniform(random_subkeys[1], (ROLLOUT_BATCH, 1, SPACE_HEADS), minval=math.log(1.0 / 50.0), maxval=math.log(1.0 / 25.0)))
    slow_rate = jax.random.uniform(random_subkeys[2], (ROLLOUT_BATCH, 1, SPACE_HEADS), minval=0.1, maxval=0.4) / SEQUENCE_LENGTH
    baseline_rate = jnp.where(fast_pick, fast_rate, slow_rate)
    block_total = SEQUENCE_LENGTH // TOK_DEV
    scale_per_block = jnp.exp(jax.random.uniform(random_subkeys[3], (ROLLOUT_BATCH, block_total, 1, SPACE_HEADS), minval=-0.7, maxval=0.7))
    scale_per_block = jnp.broadcast_to(scale_per_block, (ROLLOUT_BATCH, block_total, TOK_DEV, SPACE_HEADS)).reshape(ROLLOUT_BATCH, SEQUENCE_LENGTH, SPACE_HEADS)
    scale_per_token = jnp.exp(jax.random.uniform(random_subkeys[4], (ROLLOUT_BATCH, SEQUENCE_LENGTH, SPACE_HEADS), minval=-0.7, maxval=0.7))
    token_positions = jax.random.randint(random_subkeys[5], (ROLLOUT_BATCH, 1, 2), 0, SEQUENCE_LENGTH)
    spike_present = jnp.any(jnp.arange(SEQUENCE_LENGTH)[None, :, None] == token_positions, axis=2)
    spike_depth = jax.random.uniform(random_subkeys[6], (ROLLOUT_BATCH, SEQUENCE_LENGTH, SPACE_HEADS), minval=0.22, maxval=0.5)
    return -(baseline_rate * scale_per_block * scale_per_token) - spike_present[:, :, None].astype(jnp.float32) * spike_depth


def spiked(entries, stream_key, source, target, blocks, factor):
    owner, partner = [(jnp.arange(entries.shape[position]) // (entries.shape[position] // blocks)).reshape([-1 if axis == position else 1 for axis in range(entries.ndim)]) for position in (source, target)]
    chosen = jax.random.permutation(stream_key, blocks)[partner]
    strong = (owner == chosen) | (owner == (partner + blocks // 2) % blocks)
    return jnp.where(strong, factor * entries, entries)


def shard_levels(rng, shape, shards, smallest, high):
    level = 1.0
    for axis_at, shards_of in shards:
        steps = jax.random.uniform(jax.random.fold_in(jax.random.fold_in(rng, 6), axis_at), (shards_of,), jnp.float32, smallest / len(shards), high / len(shards))
        level = level * jnp.repeat(jnp.exp(steps), shape[axis_at] // shards_of).reshape((-1,) + (1,) * (len(shape) - 1 - axis_at))
    return level


def bell_draw(stream_key, extent, scale, bound, cuts=(), dtype=jnp.bfloat16):
    drawn = jax.random.normal(stream_key, extent, jnp.float32) * scale
    if len(cuts) > 0:
        drawn = shard_levels(stream_key, extent, cuts, -0.22, 0.18) * drawn
    return jnp.clip(drawn, min=-bound, max=bound).astype(dtype)


def noise_with(rng, extent, spread, reach, shards, heavy, kind=jnp.bfloat16):
    entries = spread * jax.random.normal(rng, extent, jnp.float32)
    if shards:
        entries = entries * shard_levels(rng, extent, shards, -0.22, 0.18)
    return jnp.clip(spiked(entries, jax.random.fold_in(rng, 3), *heavy), -reach, reach).astype(kind)


def setup_inputs(seed: int = 0) -> dict:
    streams_of = jax.random.split(jax.random.key(seed), 9)
    return {
        "tokens": noise_with(streams_of[0], (ROLLOUT_BATCH, SEQUENCE_LENGTH, D), 1.0, 16.0, ((0, 64), (1, 2)), (0, 2, 64, 4.0)),
        "values": bell_draw(streams_of[1], (ROLLOUT_BATCH, SEQUENCE_LENGTH, INNER), 1.0, 6.0, ((0, 64), (1, 2))),
        "log_decay": draw_log_decay(jax.random.fold_in(streams_of[8], 71), 0),
        "out_grad": bell_draw(streams_of[3], (ROLLOUT_BATCH, SEQUENCE_LENGTH, INNER), 1.0, 6.0, ((0, 64), (1, 2))),
        "proj_weight": bell_draw(streams_of[4], (D, PROJ), D ** -0.5, 0.09375, ((0, 64),)),
        "dt_bias": jnp.clip(jax.random.uniform(streams_of[5], (SPACE_HEADS,), jnp.float32, -4.0, -2.0), -4.0, -2.0),
        "skip": jnp.clip(jax.random.uniform(streams_of[6], (SPACE_HEADS,), jnp.float32, 0.5, 1.5), 0.5, 1.5),
        "gain": jnp.clip(1.0 + 0.1 * jax.random.normal(streams_of[7], (INNER,), jnp.float32), 0.5, 1.5),
    }


epsilon = 1e-05

def low_product(pattern, left_term, right_term):
    return jnp.einsum(pattern, left_term.astype(jnp.float32), right_term.astype(jnp.float32), precision=lax.Precision.HIGHEST)

def high_product(pattern, left_term, right_term):
    return jnp.einsum(pattern, left_term.astype(jnp.float32), right_term.astype(jnp.float32), precision=lax.Precision.HIGHEST)

def prepare(projected, values, log_decay, dt_bias):
    head_count = log_decay.shape[1]
    length = values.shape[0]
    head_width = values.shape[1] // head_count
    state_width = (projected.shape[1] - head_count) // 2
    log_total = jnp.cumsum(log_decay, axis=0)
    step_pre = projected[:, 2 * state_width:] + dt_bias[None, :]
    step_size = jax.nn.softplus(step_pre)
    write_coeff = projected[:, :state_width].astype(jnp.bfloat16)
    read_coeff = projected[:, state_width:2 * state_width].astype(jnp.bfloat16)
    scores = jnp.dot(read_coeff, write_coeff.T, preferred_element_type=jnp.float32)
    tail_decay = jnp.exp(log_total[-1][None, :] - log_total)
    weight_tail = step_size * tail_decay
    values_heads = values.reshape(length, head_count, head_width)
    scaled = (values_heads.astype(jnp.float32) * weight_tail[:, :, None]).astype(jnp.bfloat16)
    local_state = low_product('shp,sn->hpn', scaled, write_coeff)
    end_decay = jnp.exp(log_total[-1])
    return (log_total, step_pre, step_size, write_coeff, read_coeff, scores, tail_decay, weight_tail, scaled, local_state, end_decay)

def decay_mask(log_total, step_size, scores, head_start, block_heads):
    part_total = log_total[:, head_start:head_start + block_heads].T
    differ = part_total[:, :, None] - part_total[:, None, :]
    length = scores.shape[0]
    causal_mask = jnp.arange(length)[:, None] >= jnp.arange(length)[None, :]
    within = jnp.where(causal_mask[None], jnp.exp(jnp.minimum(differ, 0.0)), 0.0)
    mixing = scores[None] * within * step_size[:, head_start:head_start + block_heads].T[:, None, :]
    return (within, mixing)

def combine_outputs(prepared, values, skip, gain, state_in):
    log_total, step_size, read_coeff, scores = (prepared[0], prepared[2], prepared[4], prepared[5])
    length = values.shape[0]
    head_count = log_total.shape[1]
    head_width = values.shape[1] // head_count
    values_heads = values.reshape(length, head_count, head_width)
    block_heads = min(32, head_count)
    pieces = []
    for head_start in range(0, head_count, block_heads):
        within, mixing = decay_mask(log_total, step_size, scores, head_start, block_heads)
        pieces.append(low_product('hts,shp->thp', mixing.astype(jnp.bfloat16), values_heads[:, head_start:head_start + block_heads]))
    intra_sum = jnp.concatenate(pieces, axis=1)
    growth = jnp.exp(log_total)
    carried = growth[:, :, None] * high_product('tn,hpn->thp', read_coeff, state_in)
    pre_norm = intra_sum + carried + skip[None, :, None] * values_heads.astype(jnp.float32)
    inv_rms = lax.rsqrt(lax.optimization_barrier(jnp.mean(pre_norm * pre_norm, axis=(1, 2))) + epsilon)
    mixed = (pre_norm * inv_rms[:, None, None] * gain.reshape(head_count, head_width)[None]).astype(jnp.bfloat16)
    return (mixed.reshape(length, head_count * head_width), pre_norm, carried, inv_rms, growth)

def output_grad(out_grad, pre_norm, inv_rms, gain, growth, read_coeff):
    length, head_count, head_width = pre_norm.shape
    gained = out_grad.astype(jnp.float32).reshape(length, head_count, head_width) * gain.reshape(head_count, head_width)[None]
    inner_mean = lax.optimization_barrier(jnp.mean(gained * pre_norm, axis=(1, 2)))
    grad_pre = inv_rms[:, None, None] * gained - pre_norm * (inv_rms ** 3 * inner_mean)[:, None, None]
    grad_carried = grad_pre * growth[:, :, None]
    state_grad = high_product('thp,tn->hpn', grad_carried, read_coeff)
    return (grad_pre, grad_carried, state_grad)

def block_backward(prepared, values, skip, pre_norm, carried, grad_pre, grad_carried, state_in, later_grad):
    log_total, step_pre, step_size, write_coeff, read_coeff, scores, tail_decay, weight_tail, scaled, local_state, end_decay = prepared
    length, head_count, head_width = pre_norm.shape
    values_heads = values.reshape(length, head_count, head_width)
    grad_low = grad_pre.astype(jnp.bfloat16)
    grad_log = lax.optimization_barrier(jnp.sum(grad_pre * carried, axis=2))
    grad_read = high_product('thp,hpn->tn', grad_carried, state_in)
    grad_scores = jnp.zeros_like(scores)
    block_heads = min(32, head_count)
    value_parts, step_parts, log_parts = ([], [], [])
    for head_start in range(0, head_count, block_heads):
        within, mixing = decay_mask(log_total, step_size, scores, head_start, block_heads)
        value_part = values_heads[:, head_start:head_start + block_heads]
        grad_part = grad_low[:, head_start:head_start + block_heads]
        value_parts.append(low_product('hts,thp->shp', mixing.astype(jnp.bfloat16), grad_part))
        grad_mixing = low_product('thp,shp->hts', grad_part, value_part)
        step_block = step_size[:, head_start:head_start + block_heads].T
        kernel = grad_mixing * scores[None] * within
        step_parts.append(lax.optimization_barrier(jnp.sum(kernel, axis=1)).T)
        energy = kernel * step_block[:, None, :]
        log_parts.append((lax.optimization_barrier(jnp.sum(energy, axis=2)) - lax.optimization_barrier(jnp.sum(energy, axis=1))).T)
        grad_scores = grad_scores + lax.optimization_barrier(jnp.sum(grad_mixing * within * step_block[:, None, :], axis=0))
    grad_values = skip[None, :, None] * grad_pre + jnp.concatenate(value_parts, axis=1)
    grad_step = jnp.concatenate(step_parts, axis=1)
    grad_log = grad_log + jnp.concatenate(log_parts, axis=1)
    grad_read = grad_read + high_product('ts,sn->tn', grad_scores, write_coeff)
    grad_write = high_product('ts,tn->sn', grad_scores, read_coeff)
    grad_scaled = high_product('hpn,sn->shp', later_grad, write_coeff)
    grad_values = grad_values + grad_scaled * weight_tail[:, :, None]
    grad_weight_tail = lax.optimization_barrier(jnp.sum(grad_scaled * values_heads.astype(jnp.float32), axis=2))
    grad_write = grad_write + high_product('shp,hpn->sn', scaled, later_grad)
    grad_step = grad_step + grad_weight_tail * tail_decay
    grad_log = grad_log - grad_weight_tail * weight_tail
    grad_end = lax.optimization_barrier(jnp.sum(grad_weight_tail * weight_tail, axis=0)) + lax.optimization_barrier(jnp.sum(later_grad * state_in, axis=(1, 2))) * end_decay
    grad_log = grad_log.at[-1].add(grad_end)
    grad_decay = jnp.cumsum(grad_log[::-1], axis=0)[::-1]
    grad_step_pre = grad_step * jax.nn.sigmoid(step_pre)
    grad_projected = jnp.concatenate([grad_write, grad_read, grad_step_pre], axis=1).astype(jnp.bfloat16)
    return (grad_values.reshape(length, head_count * head_width).astype(jnp.bfloat16), grad_decay, grad_projected)

def one_rollout(token_rows, value_rows, decay_rows, grad_rows, proj_weight, dt_bias, skip, gain):
    head_count = decay_rows.shape[1]
    head_width = value_rows.shape[1] // head_count
    state_width = (proj_weight.shape[1] - head_count) // 2
    total_rows = token_rows.shape[0]
    block_count = total_rows // TOK_DEV
    projected = jnp.dot(token_rows, proj_weight, preferred_element_type=jnp.float32)
    proj_blocks = projected.reshape(block_count, TOK_DEV, projected.shape[1])
    value_blocks = value_rows.reshape(block_count, TOK_DEV, value_rows.shape[1])
    decay_blocks = decay_rows.reshape(block_count, TOK_DEV, head_count)
    grad_blocks = grad_rows.reshape(block_count, TOK_DEV, grad_rows.shape[1])
    empty_state = jnp.zeros((head_count, head_width, state_width), jnp.float32)

    def forward_chain(state_now, block):
        prepared = prepare(block[0], block[1], block[2], dt_bias)
        return (prepared[10][:, None, None] * state_now + prepared[9], state_now)
    unused, states_in = lax.scan(forward_chain, empty_state, (proj_blocks, value_blocks, decay_blocks))

    def outputs_pass(running, block):
        prepared = prepare(block[0], block[1], block[2], dt_bias)
        mixed, pre_norm, carried, inv_rms, growth = combine_outputs(prepared, block[1], skip, gain, block[4])
        grads = output_grad(block[3], pre_norm, inv_rms, gain, growth, prepared[4])
        return (running, (mixed, grads[2], prepared[10]))
    unused_too, (mixed_blocks, state_grads, end_blocks) = lax.scan(outputs_pass, jnp.zeros((), jnp.float32), (proj_blocks, value_blocks, decay_blocks, grad_blocks, states_in))

    def backward_chain(later, pair):
        return (pair[0] + pair[1][:, None, None] * later, later)
    unused_last, later_all = lax.scan(backward_chain, empty_state, (state_grads, end_blocks), reverse=True)

    def backward_pass(running, block):
        prepared = prepare(block[0], block[1], block[2], dt_bias)
        mixed, pre_norm, carried, inv_rms, growth = combine_outputs(prepared, block[1], skip, gain, block[4])
        grad_pre, grad_carried, state_grad = output_grad(block[3], pre_norm, inv_rms, gain, growth, prepared[4])
        result = block_backward(prepared, block[1], skip, pre_norm, carried, grad_pre, grad_carried, block[4], block[5])
        return (running, result)
    unused_back, (value_grads, decay_grads, proj_grads) = lax.scan(backward_pass, jnp.zeros((), jnp.float32), (proj_blocks, value_blocks, decay_blocks, grad_blocks, states_in, later_all))
    grad_projected = proj_grads.reshape(total_rows, proj_grads.shape[2])
    grad_tokens = jnp.dot(grad_projected, proj_weight.T, preferred_element_type=jnp.float32).astype(jnp.bfloat16)
    weight_term = lax.dot_general(token_rows, grad_projected, (((0,), (0,)), ((), ())), preferred_element_type=jnp.float32)
    mixed_all = mixed_blocks.reshape(total_rows, mixed_blocks.shape[2])
    value_all = value_grads.reshape(total_rows, value_grads.shape[2])
    decay_all = decay_grads.reshape(total_rows, head_count)
    return (mixed_all, grad_tokens, value_all, decay_all, weight_term)

def reference(tokens, values, log_decay, out_grad, proj_weight, dt_bias, skip, gain):

    def per_rollout(inputs):
        return one_rollout(inputs[0], inputs[1], inputs[2], inputs[3], proj_weight, dt_bias, skip, gain)
    mixed, grad_tokens, grad_values, grad_decay, weight_terms = lax.map(per_rollout, (tokens, values, log_decay, out_grad))
    grad_weight = lax.optimization_barrier(jnp.sum(weight_terms, axis=0))
    return (mixed, grad_tokens, grad_values, grad_decay, grad_weight)
```

```python
import functools

import jax
import jax.numpy as jnp
from jax import lax
from jax.experimental import pallas as pl
from jax.experimental.pallas import tpu as pltpu
from jax.sharding import PartitionSpec as P

epsilon = 1e-05
bf16, f32 = jnp.bfloat16, jnp.float32
CHUNK = 128
TILE = 1024
SUB = 256
HEADS_TILE = 16
RS1, RS2, RE1, RE2, EC1, EC2, IRS1, IEC1, LRE2, LEC2, LON = range(11)


def dot(a, b):
    return jnp.dot(a, b, preferred_element_type=f32)


def dot_nt(a, b):
    return lax.dot_general(a, b, (((1,), (1,)), ((), ())), preferred_element_type=f32)


def dot_exact(a, b):
    return lax.dot_general(
        a, b, (((1,), (0,)), ((), ())), precision=lax.Precision.HIGHEST, preferred_element_type=f32
    )


def split(x):
    high = x.astype(bf16)
    return high, (x - high.astype(f32)).astype(bf16)


def tile_heads(x, i):
    moved = pltpu.roll(x, lax.rem(128 - HEADS_TILE * i, 128), 1)
    return jnp.concatenate(split(moved), axis=1)


def chunks():
    return [(k, slice(k * CHUNK, (k + 1) * CHUNK)) for k in range(2)]


def subs():
    return [slice(j * SUB, (j + 1) * SUB) for j in range(TILE // SUB)]


def params(limit=48):
    return pltpu.CompilerParams(
        dimension_semantics=("arbitrary",), vmem_limit_bytes=limit * 2**20
    )


def cost(flops, moved):
    return pl.CostEstimate(flops=int(flops), bytes_accessed=int(moved), transcendentals=0)


def const(shape):
    return pl.BlockSpec(shape, lambda i: (0,) * len(shape))


def decay_kernel(on_ref, decay_ref, tok_ref, a_ref, b_ref, row_ref, tokt_ref):
    tokt_ref[...] = tok_ref[...].T

    @pl.when(pl.program_id(0) == 0)
    def _():
        n = decay_ref.shape[0]
        lower = lax.broadcasted_iota(jnp.int32, (n, n), 0) >= lax.broadcasted_iota(
            jnp.int32, (n, n), 1
        )
        total = dot_exact(jnp.where(lower, 1.0, 0.0).astype(f32), decay_ref[...])
        middle = [total[k * CHUNK + CHUNK // 2 - 1 :][:1] for k in range(2)]
        end = [total[(k + 1) * CHUNK - 1 :][:1] for k in range(2)]
        for k, rows in chunks():
            a_ref[rows, :] = jnp.exp(total[rows] - middle[k])
            b_ref[rows, :] = jnp.exp(middle[k] - total[rows])
        late = on_ref[0]
        early = 1.0 - late
        rs1, rs2 = jnp.exp(middle[0]), jnp.exp(middle[1] - end[0])
        re1, re2 = jnp.exp(end[0] - middle[0]), jnp.exp(end[1] - middle[1])
        ec1, ec2 = jnp.exp(end[0]), jnp.exp(end[1] - end[0])
        table = [rs1, rs2, re1, re2, ec1, ec2, rs1 * late, ec1 * late, re2 * early, ec2 * early]
        table.append(jnp.ones_like(rs1) * early)
        table += [jnp.zeros_like(rs1)] * (16 - len(table))
        row_ref[...] = jnp.concatenate(table, axis=0)


def decay_call(on, decay, tokens):
    n, heads = decay.shape
    width = tokens.shape[1]
    step = 1024
    return pl.pallas_call(
        decay_kernel,
        grid=(width // step,),
        in_specs=[
            pl.BlockSpec(memory_space=pltpu.SMEM),
            const((n, heads)),
            pl.BlockSpec((n, step), lambda i: (0, i)),
        ],
        out_specs=[
            const((n, heads)),
            const((n, heads)),
            const((16, heads)),
            pl.BlockSpec((step, n), lambda i: (i, 0)),
        ],
        out_shape=[
            jax.ShapeDtypeStruct((n, heads), f32),
            jax.ShapeDtypeStruct((n, heads), f32),
            jax.ShapeDtypeStruct((16, heads), f32),
            jax.ShapeDtypeStruct((width, n), bf16),
        ],
        compiler_params=params(),
        cost_estimate=cost(1e8, 8e6),
        name="decay",
    )(on, decay, tokens)


def project_kernel(
    half, is_ref, tok_ref, own_ref, other_ref, bias_ref, b_ref,
    full_ref, lhsy_ref, lhsu_ref, wt_ref, rt_ref, w_ref, r_ref, bs_ref, rho_ref, sc_ref, acc_ref,
):
    i = pl.program_id(0)
    first = is_ref[0] > 0.5
    own, other = own_ref[...], other_ref[...]
    groups, cols = own.shape[0] // half, own.shape[1]
    lead = jnp.where(first, other, own).reshape(groups, half, cols)
    trail = jnp.where(first, own, other).reshape(groups, half, cols)
    weight = jnp.concatenate([lead, trail], axis=1).reshape(groups * half * 2, cols)
    full_ref[...] = weight
    part = dot(tok_ref[...], weight)

    @pl.when(i == 0)
    def _():
        acc_ref[...] = part

    @pl.when(i > 0)
    def _():
        acc_ref[...] += part

    @pl.when(i == pl.num_programs(0) - 1)
    def _():
        projected = acc_ref[...]
        pre = projected[:, 256:384] + bias_ref[...]
        small = jnp.exp(-jnp.abs(pre))
        step = jnp.maximum(pre, 0.0) + jnp.log1p(small)
        sig = jnp.where(pre >= 0, 1.0, small) / (1.0 + small)
        rho_ref[...] = jnp.where(pre < -15.0, 1.0, sig / jnp.maximum(step, 1e-8))
        bs_ref[...] = step * b_ref[...]
        write = projected[:, :128].astype(bf16)
        read = projected[:, 128:256].astype(bf16)
        w_ref[...] = write
        r_ref[...] = read
        causal = lax.broadcasted_iota(jnp.int32, (CHUNK, CHUNK), 0) >= lax.broadcasted_iota(
            jnp.int32, (CHUNK, CHUNK), 1
        )
        for k, rows in chunks():
            wf, rf = write[rows].astype(f32), read[rows].astype(f32)
            scores = jnp.where(causal, dot_nt(read[rows], write[rows]), 0.0)
            most = jnp.max(jnp.max(jnp.abs(scores), axis=1, keepdims=True), axis=0, keepdims=True)
            power = jnp.exp2(jnp.ceil(jnp.log2(jnp.maximum(most, 1.0))))
            down = 1.0 / power
            lhsy_ref[k] = jnp.concatenate([scores * down, rf * down], axis=1).astype(bf16)
            lhsu_ref[k] = jnp.concatenate([scores.T * down, wf * down], axis=1).astype(bf16)
            wt_ref[k] = wf.T.astype(bf16)
            rt_ref[k] = rf.T.astype(bf16)
            sc_ref[k] = jnp.broadcast_to(power, (8, 128))


def project_call(is_first, tokens, own, other, bias, b, half):
    n, width = tokens.shape
    cols = own.shape[1]
    step = max(512, 2 * half)
    heads = b.shape[1]
    sds = jax.ShapeDtypeStruct
    return pl.pallas_call(
        functools.partial(project_kernel, half),
        grid=(width // step,),
        in_specs=[
            pl.BlockSpec(memory_space=pltpu.SMEM),
            pl.BlockSpec((n, step), lambda i: (0, i)),
            pl.BlockSpec((step // 2, cols), lambda i: (i, 0)),
            pl.BlockSpec((step // 2, cols), lambda i: (i, 0)),
            const((1, heads)),
            const((n, heads)),
        ],
        out_specs=[
            pl.BlockSpec((step, cols), lambda i: (i, 0)),
            const((2, CHUNK, 256)),
            const((2, CHUNK, 256)),
            const((2, 128, CHUNK)),
            const((2, 128, CHUNK)),
            const((n, 128)),
            const((n, 128)),
            const((n, heads)),
            const((n, heads)),
            const((2, 8, 128)),
        ],
        out_shape=[
            sds((width, cols), bf16),
            sds((2, CHUNK, 256), bf16),
            sds((2, CHUNK, 256), bf16),
            sds((2, 128, CHUNK), bf16),
            sds((2, 128, CHUNK), bf16),
            sds((n, 128), bf16),
            sds((n, 128), bf16),
            sds((n, heads), f32),
            sds((n, heads), f32),
            sds((2, 8, 128), f32),
        ],
        scratch_shapes=[pltpu.VMEM((n, cols), f32)],
        compiler_params=params(),
        cost_estimate=cost(8e8, 1e7),
        name="project",
    )(is_first, tokens, own, other, bias, b)


def state_kernel(v_ref, bs_ref, row_ref, wt_ref, e_ref, x_ref, out_ref, first_ref):
    i = pl.program_id(0)
    bs, table = tile_heads(bs_ref[...], i), tile_heads(row_ref[...], i)
    for at in subs():
        spread = e_ref[:, at]
        rf = dot(table, spread)
        local = []
        for k, rows in chunks():
            x = (v_ref[rows, at].astype(f32) * dot(bs[rows], spread)).astype(bf16)
            x_ref[rows, at] = x
            local.append(dot(wt_ref[k], x) * rf[RE1 + k : RE1 + k + 1])
        first_ref[:, at] = local[0].astype(bf16)
        out_ref[:, at] = (rf[EC2 : EC2 + 1] * local[0] + local[1]).astype(bf16)


def tiled(rows):
    return pl.BlockSpec((rows, TILE), lambda i: (0, i))


def state_call(values, bs, table, wt, spread):
    n, inner = values.shape
    sds = jax.ShapeDtypeStruct
    return pl.pallas_call(
        state_kernel,
        grid=(inner // TILE,),
        in_specs=[
            tiled(n),
            const(bs.shape),
            const(table.shape),
            const(wt.shape),
            const(spread.shape),
        ],
        out_specs=[tiled(n), tiled(128), tiled(128)],
        out_shape=[sds((n, inner), bf16), sds((128, inner), bf16), sds((128, inner), bf16)],
        compiler_params=params(),
        cost_estimate=cost(2e9, 1.3e7),
        name="states",
    )(values, bs, table, wt, spread)


def entering_states(rf, state_ref, first_ref, at):
    state = state_ref[:, at].astype(f32)
    second = rf[IEC1 : IEC1 + 1] * state + first_ref[:, at].astype(f32)
    return (
        (rf[IRS1 : IRS1 + 1] * state).astype(bf16),
        (rf[RS2 : RS2 + 1] * second).astype(bf16),
    )


def outputs_kernel(
    v_ref, o_ref, x_ref, state_ref, first_ref, a_ref, row_ref, lhsy_ref, rt_ref, sc_ref,
    skip_ref, gain_ref, e_ref, gather_ref,
    mixed_ref, g_ref, ga_ref, sgin_ref, sg2_ref, rows_ref,
    ys_ref, vs_ref, os_ref, square_ref, inner_ref, inv_ref, coef_ref,
):
    step = pl.program_id(0)
    tiles = pl.num_programs(0) // 2
    i = lax.rem(step, tiles)
    decay, table = tile_heads(a_ref[...], i), tile_heads(row_ref[...], i)

    @pl.when(step == 0)
    def _():
        square_ref[...] = jnp.zeros_like(square_ref)
        inner_ref[...] = jnp.zeros_like(inner_ref)
        rows_ref[...] = jnp.zeros_like(rows_ref)

    @pl.when(step < tiles)
    def _():
        vs_ref[i] = v_ref[...]
        os_ref[i] = o_ref[...]
        for at in subs():
            spread = e_ref[:, at]
            rf = dot(table, spread)
            entering = entering_states(rf, state_ref, first_ref, at)
            for k, rows in chunks():
                y = dot(lhsy_ref[k], jnp.concatenate([x_ref[rows, at], entering[k]], axis=0))
                ys_ref[i, rows, at] = y
                scale = sc_ref[k, 0:1, 0:1]
                pre = dot(decay[rows], spread) * y * scale
                pre += skip_ref[:, at] * v_ref[rows, at].astype(f32)
                square = pre * pre
                both = o_ref[rows, at].astype(f32) * gain_ref[:, at] * pre
                square_ref[rows, :] += square[:, :128] + square[:, 128:]
                inner_ref[rows, :] += both[:, :128] + both[:, 128:]

    @pl.when(step == tiles)
    def _():
        channels = tiles * TILE
        mean = jnp.sum(square_ref[...], axis=1, keepdims=True) / channels
        inv = lax.rsqrt(mean + epsilon)
        inner = jnp.sum(inner_ref[...], axis=1, keepdims=True) / channels
        inv_ref[...] = jnp.broadcast_to(inv, inv_ref.shape)
        coef_ref[...] = jnp.broadcast_to(inv * inv * inv * inner, coef_ref.shape)

    @pl.when(step >= tiles)
    def _():
        sums = [jnp.zeros((CHUNK, 128), f32) for _ in range(2)]
        for at in subs():
            spread = e_ref[:, at]
            rf = dot(table, spread)
            grads = []
            for k, rows in chunks():
                wide = dot(decay[rows], spread)
                y = ys_ref[i, rows, at]
                scale = sc_ref[k, 0:1, 0:1]
                pre = wide * y * scale + skip_ref[:, at] * vs_ref[i, rows, at].astype(f32)
                inv = jnp.concatenate([inv_ref[rows, :]] * 2, axis=1)
                coef = jnp.concatenate([coef_ref[rows, :]] * 2, axis=1)
                gain = gain_ref[:, at]
                g = inv * (os_ref[i, rows, at].astype(f32) * gain) - pre * coef
                mixed_ref[rows, at] = (pre * inv * gain).astype(bf16)
                g_ref[rows, at] = g.astype(bf16)
                ga = (wide * g).astype(bf16)
                ga_ref[rows, at] = ga
                high, low = split(ga.astype(f32) * y)
                gather = gather_ref[at, :]
                sums[k] += dot(high, gather) + dot(low, gather)
                grads.append(dot(rt_ref[k], ga) * rf[RS1 + k : RS1 + k + 1])
            sg2_ref[:, at] = grads[1].astype(bf16)
            sgin_ref[:, at] = (grads[0] + rf[EC1 : EC1 + 1] * grads[1]).astype(bf16)
        for k, rows in chunks():
            back = pltpu.roll(sums[k], HEADS_TILE * i, 1)
            rows_ref[rows, :] += back * sc_ref[k, 0:1, 0:1]


def outputs_call(
    values, out_grad, x, state, first, a, table, lhsy, rt, sc, skip, gain, spread, gather
):
    n, inner = values.shape
    tiles = inner // TILE
    sds = jax.ShapeDtypeStruct

    def early(rows):
        return pl.BlockSpec((rows, TILE), lambda i: (0, jnp.minimum(i, tiles - 1)))

    def late(rows):
        return pl.BlockSpec((rows, TILE), lambda i: (0, jnp.maximum(i - tiles, 0)))

    def again(rows):
        return pl.BlockSpec((rows, TILE), lambda i: (0, lax.rem(i, tiles)))

    return pl.pallas_call(
        outputs_kernel,
        grid=(2 * tiles,),
        in_specs=[
            early(n),
            early(n),
            early(n),
            early(128),
            early(128),
            const(a.shape),
            const(table.shape),
            const(lhsy.shape),
            const(rt.shape),
            const(sc.shape),
            again(1),
            again(1),
            const(spread.shape),
            const(gather.shape),
        ],
        out_specs=[late(n), late(n), late(n), late(128), late(128), const((n, 128))],
        out_shape=[
            sds((n, inner), bf16),
            sds((n, inner), bf16),
            sds((n, inner), bf16),
            sds((128, inner), bf16),
            sds((128, inner), bf16),
            sds((n, 128), f32),
        ],
        scratch_shapes=[
            pltpu.VMEM((tiles, n, TILE), f32),
            pltpu.VMEM((tiles, n, TILE), bf16),
            pltpu.VMEM((tiles, n, TILE), bf16),
            pltpu.VMEM((n, 128), f32),
            pltpu.VMEM((n, 128), f32),
            pltpu.VMEM((n, 128), f32),
            pltpu.VMEM((n, 128), f32),
        ],
        compiler_params=params(),
        cost_estimate=cost(6e9, 4e7),
        name="outputs",
    )(values, out_grad, x, state, first, a, table, lhsy, rt, sc, skip, gain, spread, gather)


def read_kernel(ga_ref, x_ref, state_ref, first_ref, row_ref, e_ref, out_ref):
    i = pl.program_id(0)
    table = tile_heads(row_ref[...], i)

    @pl.when(i == 0)
    def _():
        out_ref[...] = jnp.zeros_like(out_ref)

    for at in subs():
        rf = dot(table, e_ref[:, at])
        entering = entering_states(rf, state_ref, first_ref, at)
        for k, rows in chunks():
            right = jnp.concatenate([x_ref[rows, at], entering[k]], axis=0)
            out_ref[k] += dot_nt(ga_ref[rows, at], right)


def read_call(ga, x, state, first, table, spread):
    n, inner = ga.shape
    return pl.pallas_call(
        read_kernel,
        grid=(inner // TILE,),
        in_specs=[
            tiled(n),
            tiled(n),
            tiled(128),
            tiled(128),
            const(table.shape),
            const(spread.shape),
        ],
        out_specs=const((2, CHUNK, 256)),
        out_shape=jax.ShapeDtypeStruct((2, CHUNK, 256), f32),
        compiler_params=params(),
        cost_estimate=cost(1.2e9, 1.2e7),
        name="read_grads",
    )(ga, x, state, first, table, spread)


def backward_kernel(
    ga_ref, g_ref, x_ref, later_ref, sg2_ref, sout_ref, bs_ref, row_ref, lhsu_ref, sc_ref,
    skip_ref, e_ref, gather_ref, gsr_ref, w_ref, r_ref, rows_ref, rho_ref,
    vg_ref, gp_ref, gd_ref,
    cols_ref, gw_ref, end_ref,
):
    i = pl.program_id(0)
    bs, table = tile_heads(bs_ref[...], i), tile_heads(row_ref[...], i)

    @pl.when(i == 0)
    def _():
        cols_ref[...] = jnp.zeros_like(cols_ref)
        gw_ref[...] = jnp.zeros_like(gw_ref)
        end_ref[...] = jnp.zeros_like(end_ref)

    sums = [jnp.zeros((CHUNK, 128), f32) for _ in range(2)]
    end = jnp.zeros((16, 128), f32)
    for at in subs():
        spread, gather = e_ref[:, at], gather_ref[at, :]
        rf = dot(table, spread)
        later = later_ref[:, at].astype(f32)
        middle = sg2_ref[:, at].astype(f32) + rf[LEC2 : LEC2 + 1] * later
        leaving = [
            (rf[RE1 : RE1 + 1] * middle).astype(bf16),
            (rf[LRE2 : LRE2 + 1] * later).astype(bf16),
        ]
        both = later * sout_ref[:, at].astype(f32) * rf[LON : LON + 1]
        high, low = split(jnp.sum(both.reshape(8, 16, SUB), axis=0))
        end += dot(high, gather) + dot(low, gather)
        for k, rows in chunks():
            x = x_ref[rows, at]
            u = dot(lhsu_ref[k], jnp.concatenate([ga_ref[rows, at], leaving[k]], axis=0))
            scale = sc_ref[k, 0:1, 0:1]
            vg = dot(bs[rows], spread) * u * scale + skip_ref[:, at] * g_ref[rows, at].astype(f32)
            vg_ref[rows, at] = vg.astype(bf16)
            high, low = split(x.astype(f32) * u)
            sums[k] += dot(high, gather) + dot(low, gather)
            gw_ref[rows, :] += dot_nt(x, leaving[k])
    for k, rows in chunks():
        cols_ref[rows, :] += pltpu.roll(sums[k], HEADS_TILE * i, 1) * sc_ref[k, 0:1, 0:1]
    end_ref[...] += pltpu.roll(end, HEADS_TILE * i, 1)

    @pl.when(i == pl.num_programs(0) - 1)
    def _():
        causal = lax.broadcasted_iota(jnp.int32, (CHUNK, CHUNK), 0) >= lax.broadcasted_iota(
            jnp.int32, (CHUNK, CHUNK), 1
        )
        for k, rows in chunks():
            scores = jnp.where(causal, gsr_ref[k, :, :128], 0.0)
            read = gsr_ref[k, :, 128:] + dot(scores.astype(bf16), w_ref[rows, :])
            write = gw_ref[rows, :] + dot(scores.T.astype(bf16), r_ref[rows, :])
            gp_ref[rows, 0:128] = write.astype(bf16)
            gp_ref[rows, 128:256] = read.astype(bf16)
        cols = cols_ref[...]
        gp_ref[:, 256:384] = (cols * rho_ref[...]).astype(bf16)
        n = cols.shape[0]
        upper = lax.broadcasted_iota(jnp.int32, (n, n), 0) <= lax.broadcasted_iota(
            jnp.int32, (n, n), 1
        )
        total = dot_exact(jnp.where(upper, 1.0, 0.0).astype(f32), rows_ref[...] - cols)
        gd_ref[...] = total + jnp.sum(end_ref[...], axis=0, keepdims=True)


def backward_call(
    ga, g, x, later, sg2, sout, bs, table, lhsu, sc, skip, spread, gather, gsr, w, r, rows, rho
):
    n, inner = ga.shape
    sds = jax.ShapeDtypeStruct
    return pl.pallas_call(
        backward_kernel,
        grid=(inner // TILE,),
        in_specs=[
            tiled(n),
            tiled(n),
            tiled(n),
            tiled(128),
            tiled(128),
            tiled(128),
            const(bs.shape),
            const(table.shape),
            const(lhsu.shape),
            const(sc.shape),
            tiled(1),
            const(spread.shape),
            const(gather.shape),
            const(gsr.shape),
            const(w.shape),
            const(r.shape),
            const(rows.shape),
            const(rho.shape),
        ],
        out_specs=[tiled(n), const((n, 384)), const((n, 128))],
        out_shape=[sds((n, inner), bf16), sds((n, 384), bf16), sds((n, 128), f32)],
        scratch_shapes=[
            pltpu.VMEM((n, 128), f32),
            pltpu.VMEM((n, 128), f32),
            pltpu.VMEM((16, 128), f32),
        ],
        compiler_params=params(),
        cost_estimate=cost(4e9, 2.5e7),
        name="backward",
    )(ga, g, x, later, sg2, sout, bs, table, lhsu, sc, skip, spread, gather, gsr, w, r, rows, rho)


SWAP = [(0, 1), (1, 0)]


def on_device(tokens, values, log_decay, out_grad, proj_weight, dt_bias, skip, gain):
    tokens, values, log_decay, out_grad = tokens[0], values[0], log_decay[0], out_grad[0]
    me = lax.axis_index("ctx")
    owners = lax.axis_size("dp")
    n, inner = values.shape
    heads = log_decay.shape[1]
    half = proj_weight.shape[0] // 2
    cols = proj_weight.shape[1]

    mine = lax.dynamic_slice_in_dim(proj_weight, me * half, half, 0)
    own = lax.all_to_all(
        jnp.broadcast_to(mine[None], (owners, half, cols)), "dp", 0, 0, tiled=True
    ).reshape(owners * half, cols)
    other = lax.ppermute(own, "ctx", SWAP)

    late = me.astype(f32).reshape(1)
    a, b, table, tokens_t = decay_call(late, log_decay, tokens)
    halves = tokens_t.reshape(owners, 2, half, n)
    keep = lax.dynamic_index_in_dim(halves, me, 1, False).reshape(owners * half, n)
    give = lax.dynamic_index_in_dim(halves, 1 - me, 1, False).reshape(owners * half, n)
    got = lax.ppermute(give, "ctx", SWAP)

    lane_head = jnp.arange(TILE) // (inner // heads)
    spread = (lane_head[None, :] == (jnp.arange(256) % 128)[:, None]).astype(bf16)
    gather = (lane_head[:, None] == jnp.arange(128)[None, :]).astype(bf16)
    skip_row = jnp.repeat(skip, inner // heads)[None]

    weight, lhsy, lhsu, wt, rt, w, r, bs, rho, sc = project_call(
        late, tokens, own, other, dt_bias[None], b, half
    )
    x, sout, first = state_call(values, bs, table, wt, spread)
    state = lax.ppermute(sout, "ctx", SWAP)
    mixed, g, ga, sgin, sg2, rows = outputs_call(
        values, out_grad, x, state, first, a, table, lhsy, rt, sc, skip_row, gain[None], spread,
        gather,
    )
    later = lax.ppermute(sgin, "ctx", SWAP)
    gsr = read_call(ga, x, state, first, table, spread)
    grad_values, gp, grad_decay = backward_call(
        ga, g, x, later, sg2, sout, bs, table, lhsu, sc, skip_row, spread, gather, gsr, w, r, rows,
        rho,
    )
    gp_other = lax.ppermute(gp, "ctx", SWAP)
    term = dot(keep, gp) + dot(got, gp_other)
    parts = lax.all_to_all(
        term.astype(bf16).reshape(owners, half, cols), "dp", 0, 0, tiled=True
    )
    grad_tokens = dot_nt(gp, weight).astype(bf16)
    owned = jnp.sum(parts.astype(f32), axis=0)
    owned_other = lax.ppermute(owned, "ctx", SWAP)
    grad_weight = jnp.where(
        me == 0,
        jnp.concatenate([owned, owned_other], axis=0),
        jnp.concatenate([owned_other, owned], axis=0),
    )
    return mixed[None], grad_tokens[None], grad_values[None], grad_decay[None], grad_weight


def solution(mesh):
    rows = P("dp", "ctx", None)
    return jax.shard_map(
        on_device,
        mesh=mesh,
        in_specs=(rows, rows, rows, rows, P("dp", None), P(), P(), P()),
        out_specs=(rows, rows, rows, rows, P("dp", None)),
        check_vma=False,
    )
```

```python
import functools

import jax
import jax.numpy as jnp
from jax import lax
from jax.experimental import pallas as pl
from jax.experimental.pallas import tpu as pltpu
from jax.sharding import PartitionSpec as P

epsilon = 1e-05
bf16, f32 = jnp.bfloat16, jnp.float32
CHUNK = 128
TILE = 2048
SUB = 256
HEADS_TILE = TILE // 64
BLOCK = 32
RS1, RS2, RE1, RE2, EC1, EC2, IRS1, IEC1, LRE2, LEC2, LON = range(11)


def dot(a, b):
    return jnp.dot(a, b, preferred_element_type=f32)


def dot_nt(a, b):
    return lax.dot_general(a, b, (((1,), (1,)), ((), ())), preferred_element_type=f32)


def dot_exact(a, b):
    return lax.dot_general(
        a, b, (((1,), (0,)), ((), ())), precision=lax.Precision.HIGHEST, preferred_element_type=f32
    )


def split(x):
    high = x.astype(bf16)
    return high, (x - high.astype(f32)).astype(bf16)


def spread(x, head):
    which = lax.shift_right_logical(lax.broadcasted_iota(jnp.int32, x.shape, 1), 6) + head
    parts = [
        jnp.take_along_axis(x, which + 2 * q, axis=1, mode="promise_in_bounds") for q in range(2)
    ]
    return jnp.concatenate(parts, axis=1)


def collect(halves, gather):
    rows = halves.shape[1]
    total = dot(halves.reshape(2 * rows, SUB), gather)
    return total[:rows] + total[rows:]


def chunks():
    return [(k, slice(k * CHUNK, (k + 1) * CHUNK)) for k in range(2)]


def subs(i):
    return [
        (
            pl.ds(pl.multiple_of(i * TILE + j * SUB, SUB), SUB),
            HEADS_TILE * i + j * (SUB // 64),
            slice(j * SUB, (j + 1) * SUB),
        )
        for j in range(TILE // SUB)
    ]


def each_tile(width, body):
    def step(i, unused):
        body(i)
        return unused

    lax.fori_loop(0, width // TILE, step, 0)


def blocks(k):
    return [
        (slice(r, r + BLOCK), slice(k * CHUNK + r, k * CHUNK + r + BLOCK))
        for r in range(0, CHUNK, BLOCK)
    ]


def params(limit):
    return pltpu.CompilerParams(
        dimension_semantics=("arbitrary",), vmem_limit_bytes=limit * 2**20
    )


def near(shape, dtype=bf16):
    return pltpu.VMEM(shape, dtype)


def kept(shape):
    return pltpu.HBM(shape, bf16)


def on_chip(x):
    return pltpu.with_memory_space_constraint(x, pltpu.VMEM)


def whole(count):
    return [pl.BlockSpec(memory_space=pltpu.VMEM)] * count


def sending(buffer, out, sem, i):
    slot = lax.rem(i, 2)
    place = pl.ds(pl.multiple_of(i * TILE, TILE), TILE)
    return pltpu.make_async_copy(buffer.at[slot], out.at[:, place], sem.at[slot])


def finish(buffer, out, sem):
    steps = out.shape[1] // TILE
    for i in range(max(steps - 2, 0), steps):
        sending(buffer, out, sem, i).wait()


def loop_params(limit):
    return pltpu.CompilerParams(vmem_limit_bytes=limit * 2**20)


def cost(flops, moved):
    return pl.CostEstimate(flops=int(flops), bytes_accessed=int(moved), transcendentals=0)


def const(shape):
    return pl.BlockSpec(shape, lambda i: (0,) * len(shape))


def decay_kernel(half, on_ref, decay_ref, tok_ref, a_ref, b_ref, row_ref, keep_ref, give_ref, own_ref, other_ref):
    late = on_ref[0]
    turned = tok_ref[...].T
    groups = turned.shape[0] // (2 * half)
    turned = turned.reshape(groups, 2, half, turned.shape[1])
    flat = (groups * half, turned.shape[3])
    lead, trail = turned[:, 0].reshape(flat), turned[:, 1].reshape(flat)
    keep = jnp.where(late > 0.5, trail, lead)
    give = jnp.where(late > 0.5, lead, trail)
    keep_ref[...] = keep
    give_ref[...] = give
    own_ref[...] = keep.T
    other_ref[...] = give.T

    @pl.when(pl.program_id(0) == 0)
    def _():
        n = decay_ref.shape[0]
        lower = lax.broadcasted_iota(jnp.int32, (n, n), 0) >= lax.broadcasted_iota(
            jnp.int32, (n, n), 1
        )
        total = dot_exact(jnp.where(lower, 1.0, 0.0).astype(f32), decay_ref[...])
        middle = [total[k * CHUNK + CHUNK // 2 - 1 :][:1] for k in range(2)]
        end = [total[(k + 1) * CHUNK - 1 :][:1] for k in range(2)]
        for k, rows in chunks():
            a_ref[rows, :] = jnp.exp(total[rows] - middle[k])
            b_ref[rows, :] = jnp.exp(middle[k] - total[rows])
        early = 1.0 - late
        rs1, rs2 = jnp.exp(middle[0]), jnp.exp(middle[1] - end[0])
        re1, re2 = jnp.exp(end[0] - middle[0]), jnp.exp(end[1] - middle[1])
        ec1, ec2 = jnp.exp(end[0]), jnp.exp(end[1] - end[0])
        table = [rs1, rs2, re1, re2, ec1, ec2, rs1 * late, ec1 * late, re2 * early, ec2 * early]
        table.append(jnp.ones_like(rs1) * early)
        table += [jnp.zeros_like(rs1)] * (16 - len(table))
        row_ref[...] = jnp.concatenate(table, axis=0)


def decay_call(on, decay, tokens, half):
    n, heads = decay.shape
    width = tokens.shape[1]
    step = max(1024, 2 * half)
    sds = jax.ShapeDtypeStruct
    return pl.pallas_call(
        functools.partial(decay_kernel, half),
        grid=(width // step,),
        in_specs=[
            pl.BlockSpec(memory_space=pltpu.SMEM),
            const((n, heads)),
            pl.BlockSpec((n, step), lambda i: (0, i)),
        ],
        out_specs=[
            const((n, heads)),
            const((n, heads)),
            const((16, heads)),
            pl.BlockSpec((step // 2, n), lambda i: (i, 0)),
            pl.BlockSpec((step // 2, n), lambda i: (i, 0)),
            pl.BlockSpec((n, step // 2), lambda i: (0, i)),
            pl.BlockSpec((n, step // 2), lambda i: (0, i)),
        ],
        out_shape=[
            sds((n, heads), f32),
            sds((n, heads), f32),
            sds((16, heads), f32),
            kept((width // 2, n)),
            kept((width // 2, n)),
            sds((n, width // 2), bf16),
            sds((n, width // 2), bf16),
        ],
        compiler_params=params(24 if half > 512 else 12),
        cost_estimate=cost(1e8, 8e6),
        name="decay",
    )(on, decay, tokens)


def partial_kernel(tok_ref, weight_ref, out_ref):
    part = dot(tok_ref[...], weight_ref[...])

    @pl.when(pl.program_id(0) == 0)
    def _():
        out_ref[...] = part

    @pl.when(pl.program_id(0) > 0)
    def _():
        out_ref[...] += part


def partial_call(tokens, weight):
    n, width = tokens.shape
    cols = weight.shape[1]
    step = 1024
    return pl.pallas_call(
        partial_kernel,
        grid=(width // step,),
        in_specs=[
            pl.BlockSpec((n, step), lambda i: (0, i)),
            pl.BlockSpec((step, cols), lambda i: (i, 0)),
        ],
        out_specs=const((n, cols)),
        out_shape=jax.ShapeDtypeStruct((n, cols), f32),
        compiler_params=params(10),
        cost_estimate=cost(8e8, 4e6),
        name="project_own",
    )(tokens, weight)


def project_kernel(
    tok_ref, weight_ref, part_ref, bias_ref, b_ref,
    lhsy_ref, lhsu_ref, wt_ref, rt_ref, w_ref, r_ref, bs_ref, rho_ref, sc_ref, acc_ref,
):
    i = pl.program_id(0)
    part = dot(tok_ref[...], weight_ref[...])

    @pl.when(i == 0)
    def _():
        acc_ref[...] = part_ref[...] + part

    @pl.when(i > 0)
    def _():
        acc_ref[...] += part

    @pl.when(i == pl.num_programs(0) - 1)
    def _():
        projected = acc_ref[...]
        pre = projected[:, 256:384] + bias_ref[...]
        small = jnp.exp(-jnp.abs(pre))
        step = jnp.maximum(pre, 0.0) + jnp.log1p(small)
        sig = jnp.where(pre >= 0, 1.0, small) / (1.0 + small)
        rho_ref[...] = jnp.where(pre < -15.0, 1.0, sig / jnp.maximum(step, 1e-8))
        bs_ref[...] = step * b_ref[...]
        write = projected[:, :128].astype(bf16)
        read = projected[:, 128:256].astype(bf16)
        w_ref[...] = write
        r_ref[...] = read
        causal = lax.broadcasted_iota(jnp.int32, (CHUNK, CHUNK), 0) >= lax.broadcasted_iota(
            jnp.int32, (CHUNK, CHUNK), 1
        )
        for k, rows in chunks():
            wf, rf = write[rows].astype(f32), read[rows].astype(f32)
            scores = jnp.where(causal, dot_nt(read[rows], write[rows]), 0.0)
            most = jnp.max(jnp.max(jnp.abs(scores), axis=1, keepdims=True), axis=0, keepdims=True)
            power = jnp.exp2(jnp.ceil(jnp.log2(jnp.maximum(most, 1.0))))
            down = 1.0 / power
            lhsy_ref[k] = jnp.concatenate([scores * down, rf * down], axis=1).astype(bf16)
            lhsu_ref[k] = jnp.concatenate([scores.T * down, wf * down], axis=1).astype(bf16)
            wt_ref[k] = wf.T.astype(bf16)
            rt_ref[k] = rf.T.astype(bf16)
            sc_ref[k] = jnp.broadcast_to(power, (8, 128))


def project_call(tokens, weight, part, bias, b):
    n, width = tokens.shape
    cols = weight.shape[1]
    step = 1024
    heads = b.shape[1]
    sds = jax.ShapeDtypeStruct
    shapes = [
        sds((2, CHUNK, 256), bf16),
        sds((2, CHUNK, 256), bf16),
        sds((2, 128, CHUNK), bf16),
        sds((2, 128, CHUNK), bf16),
        sds((n, 128), bf16),
        sds((n, 128), bf16),
        sds((n, heads), f32),
        sds((n, heads), f32),
        sds((2, 8, 128), f32),
    ]
    return pl.pallas_call(
        project_kernel,
        grid=(width // step,),
        in_specs=[
            pl.BlockSpec((n, step), lambda i: (0, i)),
            pl.BlockSpec((step, cols), lambda i: (i, 0)),
            const((n, cols)),
            const((1, heads)),
            const((n, heads)),
        ],
        out_specs=[const(x.shape) for x in shapes],
        out_shape=shapes,
        scratch_shapes=[pltpu.VMEM((n, cols), f32)],
        compiler_params=params(12),
        cost_estimate=cost(8e8, 4e6),
        name="project",
    )(tokens, weight, part, bias, b)


def state_kernel(v_ref, bs_ref, row_ref, wt_ref, x_ref, out_ref, first_ref):
    def tile(i):
        for at, head, _ in subs(i):
            rf = spread(row_ref[...], head)
            local = []
            for k, rows in chunks():
                for _, r in blocks(k):
                    x = v_ref[r, at].astype(f32) * spread(bs_ref[r, :], head)
                    x_ref[r, at] = x.astype(bf16)
                local.append(dot(wt_ref[k], x_ref[rows, at]) * rf[RE1 + k : RE1 + k + 1])
            first_ref[:, at] = local[0].astype(bf16)
            out_ref[:, at] = (rf[EC2 : EC2 + 1] * local[0] + local[1]).astype(bf16)

    each_tile(v_ref.shape[1], tile)


def state_call(values, bs, table, wt):
    n, inner = values.shape
    return pl.pallas_call(
        state_kernel,
        in_specs=whole(4),
        out_specs=whole(3),
        out_shape=[near((n, inner)), near((128, inner)), near((128, inner))],
        compiler_params=loop_params(8),
        cost_estimate=cost(2e9, 1.3e7),
        name="states",
    )(on_chip(values), bs, table, wt)


def entering_states(rf, state_ref, first_ref, at):
    state = state_ref[:, at].astype(f32)
    second = rf[IEC1 : IEC1 + 1] * state + first_ref[:, at].astype(f32)
    return (
        (rf[IRS1 : IRS1 + 1] * state).astype(bf16),
        (rf[RS2 : RS2 + 1] * second).astype(bf16),
    )


def outputs_kernel(
    v_ref, o_ref, x_ref, state_ref, first_ref, a_ref, row_ref, lhsy_ref, rt_ref, sc_ref,
    skip_ref, gain_ref, gather_ref,
    mixed_ref, g_ref, ga_ref, sgin_ref, sg2_ref, rows_ref,
    ys_ref, square_ref, inner_ref, inv_ref, coef_ref, half_ref, buffer_ref, sem_ref,
):
    channels = v_ref.shape[1]
    square_ref[...] = jnp.zeros_like(square_ref)
    inner_ref[...] = jnp.zeros_like(inner_ref)
    rows_ref[...] = jnp.zeros_like(rows_ref)

    def forward(i):
        for at, head, _ in subs(i):
            rf = spread(row_ref[...], head)
            entering = entering_states(rf, state_ref, first_ref, at)
            skip, gain = skip_ref[:, at], gain_ref[:, at]
            for k, rows in chunks():
                y = dot(lhsy_ref[k], jnp.concatenate([x_ref[rows, at], entering[k]], axis=0))
                ys_ref[rows, at] = y
                scale = sc_ref[k, 0:1, 0:1]
                for p, r in blocks(k):
                    pre = spread(a_ref[r, :], head) * y[p] * scale
                    pre += skip * v_ref[r, at].astype(f32)
                    square = pre * pre
                    both = o_ref[r, at].astype(f32) * gain * pre
                    square_ref[r, :] += square[:, :128] + square[:, 128:]
                    inner_ref[r, :] += both[:, :128] + both[:, 128:]

    each_tile(channels, forward)
    mean = jnp.sum(square_ref[...], axis=1, keepdims=True) / channels
    inv = lax.rsqrt(mean + epsilon)
    inner = jnp.sum(inner_ref[...], axis=1, keepdims=True) / channels
    inv_ref[...] = jnp.broadcast_to(inv, inv_ref.shape)
    coef_ref[...] = jnp.broadcast_to(inv * inv * inv * inner, coef_ref.shape)

    def gradient(i):
        @pl.when(i >= 2)
        def _():
            sending(buffer_ref, mixed_ref, sem_ref, i - 2).wait()

        tile_ref = buffer_ref.at[lax.rem(i, 2)]
        sums = jnp.zeros((2 * CHUNK, 128), f32)
        for at, head, place in subs(i):
            rf = spread(row_ref[...], head)
            skip, gain = skip_ref[:, at], gain_ref[:, at]
            half = half_ref.at[:, :, place]
            grads = []
            for k, rows in chunks():
                scale = sc_ref[k, 0:1, 0:1]
                for _, r in blocks(k):
                    wide = spread(a_ref[r, :], head)
                    y = ys_ref[r, at]
                    pre = wide * y * scale + skip * v_ref[r, at].astype(f32)
                    inv = jnp.concatenate([inv_ref[r, :]] * 2, axis=1)
                    coef = jnp.concatenate([coef_ref[r, :]] * 2, axis=1)
                    g = inv * (o_ref[r, at].astype(f32) * gain) - pre * coef
                    tile_ref[r, place] = (pre * inv * gain).astype(bf16)
                    g_ref[r, at] = g.astype(bf16)
                    ga = (wide * g).astype(bf16)
                    ga_ref[r, at] = ga
                    half[0, r, :], half[1, r, :] = split(ga.astype(f32) * y)
                grads.append(dot(rt_ref[k], ga_ref[rows, at]) * rf[RS1 + k : RS1 + k + 1])
            sums += collect(half[...], gather_ref[place, :])
            sg2_ref[:, at] = grads[1].astype(bf16)
            sgin_ref[:, at] = (grads[0] + rf[EC1 : EC1 + 1] * grads[1]).astype(bf16)
        sending(buffer_ref, mixed_ref, sem_ref, i).start()
        back = pltpu.roll(sums, HEADS_TILE * i, 1)
        for k, rows in chunks():
            rows_ref[rows, :] += back[rows] * sc_ref[k, 0:1, 0:1]

    each_tile(channels, gradient)
    finish(buffer_ref, mixed_ref, sem_ref)


def outputs_call(
    values, out_grad, x, state, first, a, table, lhsy, rt, sc, skip, gain, gather
):
    n, inner = values.shape
    return pl.pallas_call(
        outputs_kernel,
        in_specs=whole(13),
        out_specs=[pl.BlockSpec(memory_space=pltpu.HBM), *whole(5)],
        out_shape=[
            kept((n, inner)),
            near((n, inner)),
            near((n, inner)),
            near((128, inner)),
            near((128, inner)),
            near((n, 128), f32),
        ],
        scratch_shapes=[
            pltpu.VMEM((n, inner), f32),
            pltpu.VMEM((n, 128), f32),
            pltpu.VMEM((n, 128), f32),
            pltpu.VMEM((n, 128), f32),
            pltpu.VMEM((n, 128), f32),
            pltpu.VMEM((2, n, TILE), bf16),
            pltpu.VMEM((2, n, TILE), bf16),
            pltpu.SemaphoreType.DMA((2,)),
        ],
        compiler_params=loop_params(20),
        cost_estimate=cost(6e9, 4e7),
        name="outputs",
    )(on_chip(values), on_chip(out_grad), on_chip(x), on_chip(state), on_chip(first), a, table, lhsy, rt, sc, skip, gain, gather)


def read_kernel(ga_ref, x_ref, state_ref, first_ref, row_ref, out_ref):
    out_ref[...] = jnp.zeros_like(out_ref)

    def tile(i):
        sums = [jnp.zeros((CHUNK, 256), f32) for _ in range(2)]
        for at, head, _ in subs(i):
            rf = spread(row_ref[...], head)
            entering = entering_states(rf, state_ref, first_ref, at)
            for k, rows in chunks():
                right = jnp.concatenate([x_ref[rows, at], entering[k]], axis=0)
                sums[k] += dot_nt(ga_ref[rows, at], right)
        for k in range(2):
            out_ref[k] += sums[k]

    each_tile(ga_ref.shape[1], tile)


def read_call(ga, x, state, first, table):
    return pl.pallas_call(
        read_kernel,
        in_specs=whole(5),
        out_specs=whole(1)[0],
        out_shape=near((2, CHUNK, 256), f32),
        compiler_params=loop_params(8),
        cost_estimate=cost(1.2e9, 1.2e7),
        name="read_grads",
    )(on_chip(ga), on_chip(x), on_chip(state), on_chip(first), table)


def backward_kernel(
    ga_ref, g_ref, x_ref, later_ref, sg2_ref, sout_ref, bs_ref, row_ref, lhsu_ref, sc_ref,
    skip_ref, gather_ref, gsr_ref, w_ref, r_ref, rows_ref, rho_ref,
    vg_ref, gp_ref, gd_ref,
    cols_ref, gw_ref, end_ref, half_ref, buffer_ref, sem_ref,
):
    cols_ref[...] = jnp.zeros_like(cols_ref)
    gw_ref[...] = jnp.zeros_like(gw_ref)
    end_ref[...] = jnp.zeros_like(end_ref)

    def tile(i):
        @pl.when(i >= 2)
        def _():
            sending(buffer_ref, vg_ref, sem_ref, i - 2).wait()

        tile_ref = buffer_ref.at[lax.rem(i, 2)]
        sums = jnp.zeros((2 * CHUNK, 128), f32)
        end = jnp.zeros((16, 128), f32)
        writes = [jnp.zeros((CHUNK, 128), f32) for _ in range(2)]
        for at, head, place in subs(i):
            gather = gather_ref[place, :]
            half = half_ref.at[:, :, place]
            rf = spread(row_ref[...], head)
            skip = skip_ref[:, at]
            later = later_ref[:, at].astype(f32)
            middle = sg2_ref[:, at].astype(f32) + rf[LEC2 : LEC2 + 1] * later
            leaving = [
                (rf[RE1 : RE1 + 1] * middle).astype(bf16),
                (rf[LRE2 : LRE2 + 1] * later).astype(bf16),
            ]
            both = later * sout_ref[:, at].astype(f32) * rf[LON : LON + 1]
            end += collect(jnp.stack(split(jnp.sum(both.reshape(8, 16, SUB), axis=0))), gather)
            for k, rows in chunks():
                u = dot(lhsu_ref[k], jnp.concatenate([ga_ref[rows, at], leaving[k]], axis=0))
                scale = sc_ref[k, 0:1, 0:1]
                for p, r in blocks(k):
                    vg = spread(bs_ref[r, :], head) * u[p] * scale
                    tile_ref[r, place] = (vg + skip * g_ref[r, at].astype(f32)).astype(bf16)
                    half[0, r, :], half[1, r, :] = split(x_ref[r, at].astype(f32) * u[p])
                writes[k] += dot_nt(x_ref[rows, at], leaving[k])
            sums += collect(half[...], gather)
        sending(buffer_ref, vg_ref, sem_ref, i).start()
        back = pltpu.roll(sums, HEADS_TILE * i, 1)
        for k, rows in chunks():
            cols_ref[rows, :] += back[rows] * sc_ref[k, 0:1, 0:1]
            gw_ref[rows, :] += writes[k]
        end_ref[...] += pltpu.roll(end, HEADS_TILE * i, 1)

    each_tile(ga_ref.shape[1], tile)
    finish(buffer_ref, vg_ref, sem_ref)
    causal = lax.broadcasted_iota(jnp.int32, (CHUNK, CHUNK), 0) >= lax.broadcasted_iota(
        jnp.int32, (CHUNK, CHUNK), 1
    )
    for k, rows in chunks():
        scores = jnp.where(causal, gsr_ref[k, :, :128], 0.0)
        read = gsr_ref[k, :, 128:] + dot(scores.astype(bf16), w_ref[rows, :])
        write = gw_ref[rows, :] + dot(scores.T.astype(bf16), r_ref[rows, :])
        gp_ref[rows, 0:128] = write.astype(bf16)
        gp_ref[rows, 128:256] = read.astype(bf16)
    cols = cols_ref[...]
    gp_ref[:, 256:384] = (cols * rho_ref[...]).astype(bf16)
    n = cols.shape[0]
    upper = lax.broadcasted_iota(jnp.int32, (n, n), 0) <= lax.broadcasted_iota(
        jnp.int32, (n, n), 1
    )
    total = dot_exact(jnp.where(upper, 1.0, 0.0).astype(f32), rows_ref[...] - cols)
    gd_ref[...] = total + jnp.sum(end_ref[...], axis=0, keepdims=True)


def backward_call(
    ga, g, x, later, sg2, sout, bs, table, lhsu, sc, skip, gather, gsr, w, r, rows, rho
):
    n, inner = ga.shape
    return pl.pallas_call(
        backward_kernel,
        in_specs=whole(17),
        out_specs=[pl.BlockSpec(memory_space=pltpu.HBM), *whole(2)],
        out_shape=[kept((n, inner)), near((n, 384)), jax.ShapeDtypeStruct((n, 128), f32)],
        scratch_shapes=[
            pltpu.VMEM((n, 128), f32),
            pltpu.VMEM((n, 128), f32),
            pltpu.VMEM((16, 128), f32),
            pltpu.VMEM((2, n, TILE), bf16),
            pltpu.VMEM((2, n, TILE), bf16),
            pltpu.SemaphoreType.DMA((2,)),
        ],
        compiler_params=loop_params(16),
        cost_estimate=cost(4e9, 2.5e7),
        name="backward",
    )(on_chip(ga), on_chip(g), on_chip(x), on_chip(later), on_chip(sg2), on_chip(sout), bs, table, lhsu, sc, skip, gather, gsr, w, r, rows, rho)


SWAP = [(0, 1), (1, 0)]


def on_device(tokens, values, log_decay, out_grad, proj_weight, dt_bias, skip, gain):
    tokens, values, log_decay, out_grad = tokens[0], values[0], log_decay[0], out_grad[0]
    me = lax.axis_index("ctx")
    owners = lax.axis_size("dp")
    n, inner = values.shape
    heads = log_decay.shape[1]
    half = proj_weight.shape[0] // 2
    cols = proj_weight.shape[1]

    mine = lax.dynamic_slice_in_dim(proj_weight, me * half, half, 0)
    own = lax.all_to_all(
        jnp.broadcast_to(mine[None], (owners, half, cols)), "dp", 0, 0, tiled=True
    ).reshape(owners * half, cols)

    late = me.astype(f32).reshape(1)
    a, b, table, keep, give, tok_own, tok_other = decay_call(late, log_decay, tokens, half)
    lane_head = jnp.arange(TILE) // (inner // heads)
    gather = (lane_head[:, None] == jnp.arange(128)[None, :]).astype(bf16)
    skip_row = jnp.repeat(skip, inner // heads)[None]
    own, a, b, table, keep, give, tok_own, tok_other, gather, skip_row = lax.optimization_barrier(
        (own, a, b, table, keep, give, tok_own, tok_other, gather, skip_row)
    )
    other = lax.ppermute(own, "ctx", SWAP)
    part = partial_call(tok_own, own)
    lhsy, lhsu, wt, rt, w, r, bs, rho, sc = project_call(tok_other, other, part, dt_bias[None], b)
    x, sout, first = state_call(values, bs, table, wt)
    state = lax.ppermute(sout, "ctx", SWAP)
    got = lax.ppermute(give, "ctx", SWAP)
    mixed, g, ga, sgin, sg2, rows = outputs_call(
        values, out_grad, x, state, first, a, table, lhsy, rt, sc, skip_row, gain[None], gather
    )
    later = lax.ppermute(sgin, "ctx", SWAP)
    gsr = read_call(ga, x, state, first, table)
    grad_values, gp, grad_decay = backward_call(
        ga, g, x, later, sg2, sout, bs, table, lhsu, sc, skip_row, gather, gsr, w, r, rows, rho
    )
    gp_other = lax.ppermute(gp, "ctx", SWAP)
    term = dot(keep, gp) + dot(got, gp_other)
    parts = lax.all_to_all(
        term.astype(bf16).reshape(owners, half, cols), "dp", 0, 0, tiled=True
    )
    lead = jnp.where(me == 0, own, other).reshape(owners, half, cols)
    trail = jnp.where(me == 0, other, own).reshape(owners, half, cols)
    weight = jnp.concatenate([lead, trail], axis=1).reshape(2 * owners * half, cols)
    grad_tokens = dot_nt(gp, weight).astype(bf16)
    parts, grad_tokens = lax.optimization_barrier((parts, grad_tokens))
    owned = jnp.sum(parts.astype(f32), axis=0)
    owned_other = lax.ppermute(owned, "ctx", SWAP)
    grad_weight = jnp.where(
        me == 0,
        jnp.concatenate([owned, owned_other], axis=0),
        jnp.concatenate([owned_other, owned], axis=0),
    )
    return mixed[None], grad_tokens[None], grad_values[None], grad_decay[None], grad_weight


def solution(mesh):
    rows = P("dp", "ctx", None)
    return jax.shard_map(
        on_device,
        mesh=mesh,
        in_specs=(rows, rows, rows, rows, P("dp", None), P(), P(), P()),
        out_specs=(rows, rows, rows, rows, P("dp", None)),
        check_vma=False,
    )
```

```python
import functools

import jax
import jax.numpy as jnp
from jax import lax
from jax.experimental import pallas as pl
from jax.experimental.pallas import tpu as pltpu
from jax.sharding import PartitionSpec as P

epsilon = 1e-05
bf16, f32 = jnp.bfloat16, jnp.float32
CHUNK = 128
TILE = 2048
WIDE = 4096
SUB = 256
BLOCK = 32
LAST = 1024
RS1, RS2, RE1, RE2, EC1, EC2, IRS1, IEC1, LRE2, LEC2, LON = range(11)


def dot(a, b):
    return jnp.dot(a, b, preferred_element_type=f32)


def dot_nt(a, b):
    return lax.dot_general(a, b, (((1,), (1,)), ((), ())), preferred_element_type=f32)


def dot_exact(a, b):
    return lax.dot_general(
        a, b, (((1,), (0,)), ((), ())), precision=lax.Precision.HIGHEST, preferred_element_type=f32
    )


def split(x):
    high = x.astype(bf16)
    return high, (x - high.astype(f32)).astype(bf16)


def spread(x, head):
    which = lax.shift_right_logical(lax.broadcasted_iota(jnp.int32, x.shape, 1), 6) + head
    parts = [
        jnp.take_along_axis(x, which + 2 * q, axis=1, mode="promise_in_bounds") for q in range(2)
    ]
    return jnp.concatenate(parts, axis=1)


def collect(halves, gather):
    rows = halves.shape[1]
    total = dot(halves.reshape(2 * rows, SUB), gather)
    return total[:rows] + total[rows:]


def chunks():
    return [(k, slice(k * CHUNK, (k + 1) * CHUNK)) for k in range(2)]


def subs(i, tile=TILE):
    return [
        (
            pl.ds(pl.multiple_of(i * tile + j * SUB, SUB), SUB),
            (tile * i + j * SUB) // 64,
            slice(j * SUB, (j + 1) * SUB),
        )
        for j in range(tile // SUB)
    ]


def each_tile(width, body, tile=TILE):
    def step(i, unused):
        body(i)
        return unused

    lax.fori_loop(0, width // tile, step, 0)


def blocks(k):
    return [
        (slice(r, r + BLOCK), slice(k * CHUNK + r, k * CHUNK + r + BLOCK))
        for r in range(0, CHUNK, BLOCK)
    ]


def params(limit):
    return pltpu.CompilerParams(
        dimension_semantics=("arbitrary",), vmem_limit_bytes=limit * 2**20
    )


def near(shape, dtype=bf16):
    return pltpu.VMEM(shape, dtype)


def kept(shape):
    return pltpu.HBM(shape, bf16)


def on_chip(x):
    return pltpu.with_memory_space_constraint(x, pltpu.VMEM)


def whole(count):
    return [pl.BlockSpec(memory_space=pltpu.VMEM)] * count


def sending(source, out, sem, i):
    place = pl.ds(pl.multiple_of(i * TILE, TILE), TILE)
    return pltpu.make_async_copy(source.at[:, place], out.at[:, place], sem.at[i])


def loop_params(limit):
    return pltpu.CompilerParams(vmem_limit_bytes=limit * 2**20)


def cost(flops, moved):
    return pl.CostEstimate(flops=int(flops), bytes_accessed=int(moved), transcendentals=0)


def const(shape):
    return pl.BlockSpec(shape, lambda i: (0,) * len(shape))


def decay_kernel(half, on_ref, decay_ref, tok_ref, a_ref, b_ref, row_ref, keep_ref, give_ref, own_ref, other_ref):
    late = on_ref[0]
    turned = tok_ref[...].T
    groups = turned.shape[0] // (2 * half)
    turned = turned.reshape(groups, 2, half, turned.shape[1])
    flat = (groups * half, turned.shape[3])
    lead, trail = turned[:, 0].reshape(flat), turned[:, 1].reshape(flat)
    keep = jnp.where(late > 0.5, trail, lead)
    give = jnp.where(late > 0.5, lead, trail)
    keep_ref[...] = keep
    give_ref[...] = give
    own_ref[...] = keep.T
    other_ref[...] = give.T

    @pl.when(pl.program_id(0) == 0)
    def _():
        n = decay_ref.shape[0]
        lower = lax.broadcasted_iota(jnp.int32, (n, n), 0) >= lax.broadcasted_iota(
            jnp.int32, (n, n), 1
        )
        total = dot_exact(jnp.where(lower, 1.0, 0.0).astype(f32), decay_ref[...])
        middle = [total[k * CHUNK + CHUNK // 2 - 1 :][:1] for k in range(2)]
        end = [total[(k + 1) * CHUNK - 1 :][:1] for k in range(2)]
        for k, rows in chunks():
            a_ref[rows, :] = jnp.exp(total[rows] - middle[k])
            b_ref[rows, :] = jnp.exp(middle[k] - total[rows])
        early = 1.0 - late
        rs1, rs2 = jnp.exp(middle[0]), jnp.exp(middle[1] - end[0])
        re1, re2 = jnp.exp(end[0] - middle[0]), jnp.exp(end[1] - middle[1])
        ec1, ec2 = jnp.exp(end[0]), jnp.exp(end[1] - end[0])
        table = [rs1, rs2, re1, re2, ec1, ec2, rs1 * late, ec1 * late, re2 * early, ec2 * early]
        table.append(jnp.ones_like(rs1) * early)
        table += [jnp.zeros_like(rs1)] * (16 - len(table))
        table = jnp.concatenate(table, axis=0)
        for head in range(0, table.shape[1], SUB // 64):
            row_ref[:, head * 64 : head * 64 + SUB] = spread(table, head)


def decay_call(on, decay, tokens, half, inner):
    n, heads = decay.shape
    width = tokens.shape[1]
    step = max(1024, 2 * half)
    sds = jax.ShapeDtypeStruct
    return pl.pallas_call(
        functools.partial(decay_kernel, half),
        grid=(width // step,),
        in_specs=[
            pl.BlockSpec(memory_space=pltpu.SMEM),
            const((n, heads)),
            pl.BlockSpec((n, step), lambda i: (0, i)),
        ],
        out_specs=[
            const((n, heads)),
            const((n, heads)),
            const((16, inner)),
            pl.BlockSpec((step // 2, n), lambda i: (i, 0)),
            pl.BlockSpec((step // 2, n), lambda i: (i, 0)),
            pl.BlockSpec((n, step // 2), lambda i: (0, i)),
            pl.BlockSpec((n, step // 2), lambda i: (0, i)),
        ],
        out_shape=[
            near((n, heads), f32),
            near((n, heads), f32),
            near((16, inner), f32),
            near((width // 2, n)),
            kept((width // 2, n)),
            near((n, width // 2)),
            near((n, width // 2)),
        ],
        compiler_params=params(24 if half > 512 else 12),
        cost_estimate=cost(1e8, 8e6),
        name="decay",
    )(on, decay, tokens)


def partial_kernel(tok_ref, weight_ref, out_ref):
    part = dot(tok_ref[...], weight_ref[...])

    @pl.when(pl.program_id(0) == 0)
    def _():
        out_ref[...] = part

    @pl.when(pl.program_id(0) > 0)
    def _():
        out_ref[...] += part


def partial_call(tokens, weight):
    n, width = tokens.shape
    cols = weight.shape[1]
    step = 1024
    return pl.pallas_call(
        partial_kernel,
        grid=(width // step,),
        in_specs=[
            pl.BlockSpec((n, step), lambda i: (0, i)),
            pl.BlockSpec((step, cols), lambda i: (i, 0)),
        ],
        out_specs=const((n, cols)),
        out_shape=jax.ShapeDtypeStruct((n, cols), f32),
        compiler_params=params(10),
        cost_estimate=cost(8e8, 4e6),
        name="project_own",
    )(tokens, weight)


def project_kernel(
    tok_ref, weight_ref, part_ref, bias_ref, b_ref,
    lhsy_ref, lhsu_ref, wt_ref, rt_ref, w_ref, r_ref, bs_ref, rho_ref, sc_ref, acc_ref,
):
    i = pl.program_id(0)
    part = dot(tok_ref[...], weight_ref[...])

    @pl.when(i == 0)
    def _():
        acc_ref[...] = part_ref[...] + part

    @pl.when(i > 0)
    def _():
        acc_ref[...] += part

    @pl.when(i == pl.num_programs(0) - 1)
    def _():
        projected = acc_ref[...]
        pre = projected[:, 256:384] + bias_ref[...]
        small = jnp.exp(-jnp.abs(pre))
        step = jnp.maximum(pre, 0.0) + jnp.log1p(small)
        sig = jnp.where(pre >= 0, 1.0, small) / (1.0 + small)
        rho_ref[...] = jnp.where(pre < -15.0, 1.0, sig / jnp.maximum(step, 1e-8))
        bs_ref[...] = step * b_ref[...]
        write = projected[:, :128].astype(bf16)
        read = projected[:, 128:256].astype(bf16)
        w_ref[...] = write
        r_ref[...] = read
        causal = lax.broadcasted_iota(jnp.int32, (CHUNK, CHUNK), 0) >= lax.broadcasted_iota(
            jnp.int32, (CHUNK, CHUNK), 1
        )
        for k, rows in chunks():
            wf, rf = write[rows].astype(f32), read[rows].astype(f32)
            scores = jnp.where(causal, dot_nt(read[rows], write[rows]), 0.0)
            most = jnp.max(jnp.max(jnp.abs(scores), axis=1, keepdims=True), axis=0, keepdims=True)
            power = jnp.exp2(jnp.ceil(jnp.log2(jnp.maximum(most, 1.0))))
            down = 1.0 / power
            lhsy_ref[k] = jnp.concatenate([scores * down, rf * down], axis=1).astype(bf16)
            lhsu_ref[k] = jnp.concatenate([scores.T * down, wf * down], axis=1).astype(bf16)
            wt_ref[k] = wf.T.astype(bf16)
            rt_ref[k] = rf.T.astype(bf16)
            sc_ref[k] = jnp.broadcast_to(power, (8, 128))


def project_call(tokens, weight, part, bias, b):
    n, width = tokens.shape
    cols = weight.shape[1]
    step = 1024
    heads = b.shape[1]
    sds = jax.ShapeDtypeStruct
    shapes = [
        sds((2, CHUNK, 256), bf16),
        sds((2, CHUNK, 256), bf16),
        sds((2, 128, CHUNK), bf16),
        sds((2, 128, CHUNK), bf16),
        sds((n, 128), bf16),
        sds((n, 128), bf16),
        sds((n, heads), f32),
        sds((n, heads), f32),
        sds((2, 8, 128), f32),
    ]
    return pl.pallas_call(
        project_kernel,
        grid=(width // step,),
        in_specs=[
            pl.BlockSpec((n, step), lambda i: (0, i)),
            pl.BlockSpec((step, cols), lambda i: (i, 0)),
            const((n, cols)),
            const((1, heads)),
            const((n, heads)),
        ],
        out_specs=[const(x.shape) for x in shapes],
        out_shape=shapes,
        scratch_shapes=[pltpu.VMEM((n, cols), f32)],
        compiler_params=params(12),
        cost_estimate=cost(8e8, 4e6),
        name="project",
    )(tokens, weight, part, bias, b)


def state_kernel(v_ref, bs_ref, row_ref, wt_ref, x_ref, out_ref, first_ref):
    def tile(i):
        for at, head, _ in subs(i, WIDE):
            rf = row_ref[:, at]
            local = []
            for k, rows in chunks():
                x = (v_ref[rows, at].astype(f32) * spread(bs_ref[rows, :], head)).astype(bf16)
                x_ref[rows, at] = x
                local.append(dot(wt_ref[k], x) * rf[RE1 + k : RE1 + k + 1])
            first_ref[:, at] = local[0].astype(bf16)
            out_ref[:, at] = (rf[EC2 : EC2 + 1] * local[0] + local[1]).astype(bf16)

    each_tile(v_ref.shape[1], tile, WIDE)


def state_call(values, bs, table, wt):
    n, inner = values.shape
    return pl.pallas_call(
        state_kernel,
        in_specs=whole(4),
        out_specs=whole(3),
        out_shape=[near((n, inner)), near((128, inner)), near((128, inner))],
        compiler_params=loop_params(8),
        cost_estimate=cost(2e9, 1.3e7),
        name="states",
    )(on_chip(values), bs, table, wt)


def entering_states(rf, state_ref, first_ref, at):
    state = state_ref[:, at].astype(f32)
    second = rf[IEC1 : IEC1 + 1] * state + first_ref[:, at].astype(f32)
    return (
        (rf[IRS1 : IRS1 + 1] * state).astype(bf16),
        (rf[RS2 : RS2 + 1] * second).astype(bf16),
    )


def outputs_kernel(
    v_ref, o_ref, x_ref, state_ref, first_ref, a_ref, row_ref, lhsy_ref, rt_ref, sc_ref,
    skip_ref, gain_ref, gather_ref,
    out_ref, ga_ref, sgin_ref, sg2_ref, stats_ref,
    pre_ref, ys_ref, square_ref, inner_ref, half_ref, sem_ref,
):
    channels = v_ref.shape[1]
    rows_ref, inv_ref, coef_ref = (stats_ref.at[k] for k in range(3))
    square_ref[...] = jnp.zeros_like(square_ref)
    inner_ref[...] = jnp.zeros_like(inner_ref)
    rows_ref[...] = jnp.zeros_like(rows_ref)

    def forward(i):
        for at, head, _ in subs(i):
            entering = entering_states(row_ref[:, at], state_ref, first_ref, at)
            skip, gain = skip_ref[:, at], gain_ref[:, at]
            for k, rows in chunks():
                y = dot(lhsy_ref[k], jnp.concatenate([x_ref[rows, at], entering[k]], axis=0))
                ys_ref[rows, at] = y
                scale = sc_ref[k, 0:1, 0:1]
                for p, r in blocks(k):
                    pre = spread(a_ref[r, :], head) * y[p] * scale
                    pre += skip * v_ref[r, at].astype(f32)
                    pre_ref[r, at] = pre
                    square = pre * pre
                    both = o_ref[r, at].astype(f32) * gain * pre
                    square_ref[r, :] += square[:, :128] + square[:, 128:]
                    inner_ref[r, :] += both[:, :128] + both[:, 128:]
        sending(pre_ref, out_ref, sem_ref, i).start()

    each_tile(channels, forward)
    mean = jnp.sum(square_ref[...], axis=1, keepdims=True) / channels
    inv = lax.rsqrt(mean + epsilon)
    inner = jnp.sum(inner_ref[...], axis=1, keepdims=True) / channels
    inv_ref[...] = jnp.broadcast_to(inv, inv_ref.shape)
    coef_ref[...] = jnp.broadcast_to(inv * inv * inv * inner, coef_ref.shape)

    def gradient(i):
        sums = jnp.zeros((2 * CHUNK, 128), f32)
        for at, head, place in subs(i):
            rf = row_ref[:, at]
            gain = gain_ref[:, at]
            half = half_ref.at[:, :, place]
            grads = []
            for k, rows in chunks():
                for _, r in blocks(k):
                    g = grad_pre(o_ref, pre_ref, inv_ref, coef_ref, gain, r, at)
                    ga = (spread(a_ref[r, :], head) * g).astype(bf16)
                    ga_ref[r, at] = ga
                    half[0, r, :], half[1, r, :] = split(ga.astype(f32) * ys_ref[r, at])
                grads.append(dot(rt_ref[k], ga_ref[rows, at]) * rf[RS1 + k : RS1 + k + 1])
            sums += collect(half[...], gather_ref[place, :])
            sg2_ref[:, at] = grads[1].astype(bf16)
            sgin_ref[:, at] = (grads[0] + rf[EC1 : EC1 + 1] * grads[1]).astype(bf16)
        back = pltpu.roll(sums, TILE // 64 * i, 1)
        for k, rows in chunks():
            rows_ref[rows, :] += back[rows] * sc_ref[k, 0:1, 0:1]

    each_tile(channels, gradient)
    for i in range(channels // TILE):
        sending(pre_ref, out_ref, sem_ref, i).wait()


def grad_pre(o_ref, pre_ref, inv_ref, coef_ref, gain, r, at):
    inv = jnp.concatenate([inv_ref[r, :]] * 2, axis=1)
    coef = jnp.concatenate([coef_ref[r, :]] * 2, axis=1)
    return inv * (o_ref[r, at].astype(f32) * gain) - pre_ref[r, at] * coef


def outputs_call(
    values, out_grad, x, state, first, a, table, lhsy, rt, sc, skip, gain, gather
):
    n, inner = values.shape
    return pl.pallas_call(
        outputs_kernel,
        in_specs=whole(13),
        out_specs=[pl.BlockSpec(memory_space=pltpu.HBM), *whole(4)],
        out_shape=[
            pltpu.HBM((n, inner), f32),
            near((n, inner)),
            near((128, inner)),
            near((128, inner)),
            near((3, n, 128), f32),
        ],
        scratch_shapes=[
            pltpu.VMEM((n, inner), f32),
            pltpu.VMEM((n, inner), f32),
            pltpu.VMEM((n, 128), f32),
            pltpu.VMEM((n, 128), f32),
            pltpu.VMEM((2, n, TILE), bf16),
            pltpu.SemaphoreType.DMA((inner // TILE,)),
        ],
        compiler_params=loop_params(24),
        cost_estimate=cost(6e9, 4e7),
        name="outputs",
    )(on_chip(values), on_chip(out_grad), on_chip(x), on_chip(state), on_chip(first), a, table, lhsy, rt, sc, skip, gain, gather)


def read_kernel(ga_ref, x_ref, state_ref, first_ref, row_ref, out_ref):
    out_ref[...] = jnp.zeros_like(out_ref)

    def tile(i):
        sums = [jnp.zeros((CHUNK, 256), f32) for _ in range(2)]
        for at, _, _ in subs(i, WIDE):
            rf = row_ref[:, at]
            entering = entering_states(rf, state_ref, first_ref, at)
            for k, rows in chunks():
                right = jnp.concatenate([x_ref[rows, at], entering[k]], axis=0)
                sums[k] += dot_nt(ga_ref[rows, at], right)
        for k in range(2):
            out_ref[k] += sums[k]

    each_tile(ga_ref.shape[1], tile, WIDE)


def read_call(ga, x, state, first, table):
    return pl.pallas_call(
        read_kernel,
        in_specs=whole(5),
        out_specs=whole(1)[0],
        out_shape=near((2, CHUNK, 256), f32),
        compiler_params=loop_params(8),
        cost_estimate=cost(1.2e9, 1.2e7),
        name="read_grads",
    )(on_chip(ga), on_chip(x), on_chip(state), on_chip(first), table)


def leaving_states(rf, later, sg2_ref, at):
    middle = sg2_ref[:, at].astype(f32) + rf[LEC2 : LEC2 + 1] * later
    return [
        (rf[RE1 : RE1 + 1] * middle).astype(bf16),
        (rf[LRE2 : LRE2 + 1] * later).astype(bf16),
    ]


def backward_kernel(
    ga_ref, x_ref, later_ref, sg2_ref, sout_ref, row_ref, lhsu_ref, sc_ref,
    gather_ref, gsr_ref, w_ref, r_ref, rho_ref,
    gp_ref, sums_ref,
    gw_ref, half_ref,
):
    n = ga_ref.shape[0]
    cols_ref, end_ref = sums_ref.at[:n], sums_ref.at[n:]
    sums_ref[...] = jnp.zeros_like(sums_ref)
    gw_ref[...] = jnp.zeros_like(gw_ref)

    def tile(i):
        sums = jnp.zeros((n + 16, 128), f32)
        writes = jnp.zeros((n, 256), f32)
        for at, _, place in subs(i, WIDE):
            half = half_ref.at[:, :, place]
            rf = row_ref[:, at]
            later = later_ref[:, at].astype(f32)
            leaving = leaving_states(rf, later, sg2_ref, at)
            both = later * sout_ref[:, at].astype(f32) * rf[LON : LON + 1]
            half[0, n:, :], half[1, n:, :] = split(jnp.sum(both.reshape(8, 16, SUB), axis=0))
            for k, rows in chunks():
                u = dot(lhsu_ref[k], jnp.concatenate([ga_ref[rows, at], leaving[k]], axis=0))
                for p, r in blocks(k):
                    half[0, r, :], half[1, r, :] = split(x_ref[r, at].astype(f32) * u[p])
            writes += dot_nt(x_ref[:, at], jnp.concatenate(leaving, axis=0))
            sums += collect(half[...], gather_ref[place, :])
        back = pltpu.roll(sums, WIDE // 64 * i, 1)
        for k, rows in chunks():
            cols_ref[rows, :] += back[rows] * sc_ref[k, 0:1, 0:1]
            gw_ref[rows, :] += writes[rows, 128 * k : 128 * k + 128]
        end_ref[...] += back[n:]

    each_tile(ga_ref.shape[1], tile, WIDE)
    causal = lax.broadcasted_iota(jnp.int32, (CHUNK, CHUNK), 0) >= lax.broadcasted_iota(
        jnp.int32, (CHUNK, CHUNK), 1
    )
    for k, rows in chunks():
        scores = jnp.where(causal, gsr_ref[k, :, :128], 0.0)
        read = gsr_ref[k, :, 128:] + dot(scores.astype(bf16), w_ref[rows, :])
        write = gw_ref[rows, :] + dot(scores.T.astype(bf16), r_ref[rows, :])
        gp_ref[rows, 0:128] = write.astype(bf16)
        gp_ref[rows, 128:256] = read.astype(bf16)
    gp_ref[:, 256:384] = (cols_ref[...] * rho_ref[...]).astype(bf16)


def backward_call(ga, x, later, sg2, sout, table, lhsu, sc, gather, gsr, w, r, rho):
    n, inner = ga.shape
    return pl.pallas_call(
        backward_kernel,
        in_specs=whole(13),
        out_specs=whole(2),
        out_shape=[near((n, 384)), near((n + 16, 128), f32)],
        scratch_shapes=[pltpu.VMEM((n, 128), f32), pltpu.VMEM((2, n + 16, WIDE), bf16)],
        compiler_params=loop_params(14),
        cost_estimate=cost(4e9, 2.5e7),
        name="backward",
    )(on_chip(ga), on_chip(x), on_chip(later), on_chip(sg2), on_chip(sout), table, lhsu, sc, gather, gsr, w, r, rho)


def finish_kernel(
    o_ref, pre_ref, ga_ref, later_ref, sg2_ref, row_ref, skip_ref, gain_ref,
    lhsu_ref, bs_ref, sc_ref, stats_ref, sums_ref,
    mixed_ref, vg_ref, gd_ref,
):
    i = pl.program_id(0)
    rows_ref, inv_ref, coef_ref = (stats_ref.at[k] for k in range(3))
    for j in range(LAST // SUB):
        at = slice(j * SUB, (j + 1) * SUB)
        head = (LAST * i + j * SUB) // 64
        leaving = leaving_states(row_ref[:, at], later_ref[:, at].astype(f32), sg2_ref, at)
        skip, gain = skip_ref[:, at], gain_ref[:, at]
        for k, rows in chunks():
            u = dot(lhsu_ref[k], jnp.concatenate([ga_ref[rows, at], leaving[k]], axis=0))
            scale = sc_ref[k, 0:1, 0:1]
            for p, r in blocks(k):
                inv = jnp.concatenate([inv_ref[r, :]] * 2, axis=1)
                mixed_ref[r, at] = (pre_ref[r, at] * inv * gain).astype(bf16)
                g = grad_pre(o_ref, pre_ref, inv_ref, coef_ref, gain, r, at)
                vg = spread(bs_ref[r, :], head) * u[p] * scale + skip * g
                vg_ref[r, at] = vg.astype(bf16)

    @pl.when(i == pl.num_programs(0) - 1)
    def _():
        n = rows_ref.shape[0]
        upper = lax.broadcasted_iota(jnp.int32, (n, n), 0) <= lax.broadcasted_iota(
            jnp.int32, (n, n), 1
        )
        change = rows_ref[...] - sums_ref[:n, :]
        total = dot_exact(jnp.where(upper, 1.0, 0.0).astype(f32), change)
        gd_ref[...] = total + jnp.sum(sums_ref[n:, :], axis=0, keepdims=True)


def finish_call(
    out_grad, pre, ga, later, sg2, table, skip, gain, lhsu, bs, sc, stats, sums
):
    n, inner = ga.shape

    def tiled(rows):
        return pl.BlockSpec((rows, LAST), lambda i: (0, i))

    return pl.pallas_call(
        finish_kernel,
        grid=(inner // LAST,),
        in_specs=[
            tiled(n),
            tiled(n),
            tiled(n),
            tiled(128),
            tiled(128),
            tiled(16),
            tiled(1),
            tiled(1),
            const(lhsu.shape),
            const(bs.shape),
            const(sc.shape),
            const(stats.shape),
            const(sums.shape),
        ],
        out_specs=[tiled(n), tiled(n), const((n, 128))],
        out_shape=[kept((n, inner)), kept((n, inner)), jax.ShapeDtypeStruct((n, 128), f32)],
        compiler_params=params(14),
        cost_estimate=cost(3e9, 2e7),
        name="finish",
    )(out_grad, pre, ga, later, sg2, table, skip, gain, lhsu, bs, sc, stats, sums)


def term_kernel(tok_ref, gp_ref, *refs):
    out_ref = refs[-1]
    for start in range(0, tok_ref.shape[0], 256):
        at = slice(start, start + 256)
        part = dot(tok_ref[at, :], gp_ref[...])
        if len(refs) > 1:
            part += refs[0][at, :]
        out_ref[at, :] = part.astype(out_ref.dtype)


def term_call(tok, gp, *before):
    shape = (tok.shape[0], gp.shape[1])
    out = jax.ShapeDtypeStruct(shape, bf16) if before else near(shape, f32)
    return pl.pallas_call(
        term_kernel,
        in_specs=whole(2 + len(before)),
        out_specs=whole(1)[0],
        out_shape=out,
        compiler_params=loop_params(8),
        cost_estimate=cost(8e8, 3e6),
        name="term_other" if before else "term_own",
    )(tok, gp, *before)


SWAP = [(0, 1), (1, 0)]


def on_device(tokens, values, log_decay, out_grad, proj_weight, dt_bias, skip, gain):
    tokens, values, log_decay, out_grad = tokens[0], values[0], log_decay[0], out_grad[0]
    me = lax.axis_index("ctx")
    owners = lax.axis_size("dp")
    n, inner = values.shape
    heads = log_decay.shape[1]
    half = proj_weight.shape[0] // 2
    cols = proj_weight.shape[1]

    mine = lax.dynamic_slice_in_dim(proj_weight, me * half, half, 0)
    own = lax.all_to_all(
        jnp.broadcast_to(mine[None], (owners, half, cols)), "dp", 0, 0, tiled=True
    ).reshape(owners * half, cols)

    late = me.astype(f32).reshape(1)
    a, b, table, keep, give, tok_own, tok_other = decay_call(
        late, log_decay, tokens, half, inner
    )
    lane_head = jnp.arange(WIDE) // (inner // heads)
    gather = (lane_head[:, None] == jnp.arange(128)[None, :]).astype(bf16)
    skip_row = jnp.repeat(skip, inner // heads)[None]
    own, a, b, table, keep, give, tok_own, tok_other, gather, skip_row = lax.optimization_barrier(
        (own, a, b, table, keep, give, tok_own, tok_other, gather, skip_row)
    )
    other = lax.ppermute(own, "ctx", SWAP)
    part = partial_call(tok_own, own)
    lhsy, lhsu, wt, rt, w, r, bs, rho, sc = project_call(tok_other, other, part, dt_bias[None], b)
    x, sout, first = state_call(values, bs, table, wt)
    state = lax.ppermute(sout, "ctx", SWAP)
    got = lax.ppermute(give, "ctx", SWAP)
    pre, ga, sgin, sg2, stats = outputs_call(
        values, out_grad, x, state, first, a, table, lhsy, rt, sc, skip_row, gain[None], gather
    )
    later = lax.ppermute(sgin, "ctx", SWAP)
    gsr = read_call(ga, x, state, first, table)
    gp, sums = backward_call(
        ga, x, later, sg2, sout, table, lhsu, sc, gather, gsr, w, r, rho
    )
    gp_other = lax.ppermute(gp, "ctx", SWAP)
    term = term_call(on_chip(got), gp_other, term_call(keep, gp))
    parts = lax.all_to_all(term.reshape(owners, half, cols), "dp", 0, 0, tiled=True)
    mixed, grad_values, grad_decay = finish_call(
        out_grad, pre, ga, later, sg2, table, skip_row, gain[None], lhsu, bs, sc, stats, sums
    )
    lead = jnp.where(me == 0, own, other).reshape(owners, half, cols)
    trail = jnp.where(me == 0, other, own).reshape(owners, half, cols)
    weight = jnp.concatenate([lead, trail], axis=1).reshape(2 * owners * half, cols)
    grad_tokens = dot_nt(gp, weight).astype(bf16)
    parts, grad_tokens, mixed, grad_values, grad_decay = lax.optimization_barrier(
        (parts, grad_tokens, mixed, grad_values, grad_decay)
    )
    owned = jnp.sum(parts.astype(f32), axis=0)
    owned_other = lax.ppermute(owned, "ctx", SWAP)
    grad_weight = jnp.where(
        me == 0,
        jnp.concatenate([owned, owned_other], axis=0),
        jnp.concatenate([owned_other, owned], axis=0),
    )
    return mixed[None], grad_tokens[None], grad_values[None], grad_decay[None], grad_weight


def solution(mesh):
    rows = P("dp", "ctx", None)
    return jax.shard_map(
        on_device,
        mesh=mesh,
        in_specs=(rows, rows, rows, rows, P("dp", None), P(), P(), P()),
        out_specs=(rows, rows, rows, rows, P("dp", None)),
        check_vma=False,
    )
```

```python
import functools

import jax
import jax.numpy as jnp
from jax import lax
from jax.experimental import pallas as pl
from jax.experimental.pallas import tpu as pltpu
from jax.sharding import PartitionSpec as P

epsilon = 1e-05
bf16, f32 = jnp.bfloat16, jnp.float32
CHUNK = 128
TILE = 2048
WIDE = 4096
SUB = 256
BLOCK = 32
LAST = 1024
RS1, RS2, RE1, RE2, EC1, EC2, IRS1, IEC1, LRE2, LEC2, LON = range(11)


def dot(a, b):
    return jnp.dot(a, b, preferred_element_type=f32)


def dot_nt(a, b):
    return lax.dot_general(a, b, (((1,), (1,)), ((), ())), preferred_element_type=f32)


def dot_exact(a, b):
    return lax.dot_general(
        a, b, (((1,), (0,)), ((), ())), precision=lax.Precision.HIGHEST, preferred_element_type=f32
    )


def split(x):
    high = x.astype(bf16)
    return high, (x - high.astype(f32)).astype(bf16)


def spread(x, head):
    which = lax.shift_right_logical(lax.broadcasted_iota(jnp.int32, x.shape, 1), 6) + head
    parts = [
        jnp.take_along_axis(x, which + 2 * q, axis=1, mode="promise_in_bounds") for q in range(2)
    ]
    return jnp.concatenate(parts, axis=1)


def collect(halves, gather):
    rows = halves.shape[1]
    total = dot(halves.reshape(2 * rows, SUB), gather)
    return total[:rows] + total[rows:]


def chunks():
    return [(k, slice(k * CHUNK, (k + 1) * CHUNK)) for k in range(2)]


def subs(i, tile=TILE):
    return [
        (
            pl.ds(pl.multiple_of(i * tile + j * SUB, SUB), SUB),
            (tile * i + j * SUB) // 64,
            slice(j * SUB, (j + 1) * SUB),
        )
        for j in range(tile // SUB)
    ]


def each_tile(width, body, tile=TILE):
    def step(i, unused):
        body(i)
        return unused

    lax.fori_loop(0, width // tile, step, 0)


def blocks(k):
    return [
        (slice(r, r + BLOCK), slice(k * CHUNK + r, k * CHUNK + r + BLOCK))
        for r in range(0, CHUNK, BLOCK)
    ]


def params(limit):
    return pltpu.CompilerParams(
        dimension_semantics=("arbitrary",), vmem_limit_bytes=limit * 2**20
    )


def near(shape, dtype=bf16):
    return pltpu.VMEM(shape, dtype)


def kept(shape):
    return pltpu.HBM(shape, bf16)


def on_chip(x):
    return pltpu.with_memory_space_constraint(x, pltpu.VMEM)


def in_hbm(x):
    return pltpu.with_memory_space_constraint(x, pltpu.HBM)


def whole(count):
    return [pl.BlockSpec(memory_space=pltpu.VMEM)] * count


def sending(source, out, sem, i):
    place = pl.ds(pl.multiple_of(i * TILE, TILE), TILE)
    return pltpu.make_async_copy(source.at[:, place], out.at[:, place], sem.at[i])


def loop_params(limit):
    return pltpu.CompilerParams(vmem_limit_bytes=limit * 2**20)


def cost(flops, moved):
    return pl.CostEstimate(flops=int(flops), bytes_accessed=int(moved), transcendentals=0)


def const(shape):
    return pl.BlockSpec(shape, lambda i: (0,) * len(shape))


def decay_kernel(half, on_ref, decay_ref, tok_ref, a_ref, b_ref, row_ref, keep_ref, give_ref, own_ref, other_ref):
    late = on_ref[0]
    turned = tok_ref[...].T
    groups = turned.shape[0] // (2 * half)
    turned = turned.reshape(groups, 2, half, turned.shape[1])
    flat = (groups * half, turned.shape[3])
    lead, trail = turned[:, 0].reshape(flat), turned[:, 1].reshape(flat)
    keep = jnp.where(late > 0.5, trail, lead)
    give = jnp.where(late > 0.5, lead, trail)
    keep_ref[...] = keep
    give_ref[...] = give
    own_ref[...] = keep.T
    other_ref[...] = give.T

    @pl.when(pl.program_id(0) == 0)
    def _():
        n = decay_ref.shape[0]
        lower = lax.broadcasted_iota(jnp.int32, (n, n), 0) >= lax.broadcasted_iota(
            jnp.int32, (n, n), 1
        )
        total = dot_exact(jnp.where(lower, 1.0, 0.0).astype(f32), decay_ref[...])
        middle = [total[k * CHUNK + CHUNK // 2 - 1 :][:1] for k in range(2)]
        end = [total[(k + 1) * CHUNK - 1 :][:1] for k in range(2)]
        for k, rows in chunks():
            a_ref[rows, :] = jnp.exp(total[rows] - middle[k])
            b_ref[rows, :] = jnp.exp(middle[k] - total[rows])
        early = 1.0 - late
        rs1, rs2 = jnp.exp(middle[0]), jnp.exp(middle[1] - end[0])
        re1, re2 = jnp.exp(end[0] - middle[0]), jnp.exp(end[1] - middle[1])
        ec1, ec2 = jnp.exp(end[0]), jnp.exp(end[1] - end[0])
        table = [rs1, rs2, re1, re2, ec1, ec2, rs1 * late, ec1 * late, re2 * early, ec2 * early]
        table.append(jnp.ones_like(rs1) * early)
        table += [jnp.zeros_like(rs1)] * (16 - len(table))
        table = jnp.concatenate(table, axis=0)
        for head in range(0, table.shape[1], SUB // 64):
            row_ref[:, head * 64 : head * 64 + SUB] = spread(table, head)


def decay_call(on, decay, tokens, half, inner):
    n, heads = decay.shape
    width = tokens.shape[1]
    step = max(1024, 2 * half)
    sds = jax.ShapeDtypeStruct
    return pl.pallas_call(
        functools.partial(decay_kernel, half),
        grid=(width // step,),
        in_specs=[
            pl.BlockSpec(memory_space=pltpu.SMEM),
            const((n, heads)),
            pl.BlockSpec((n, step), lambda i: (0, i)),
        ],
        out_specs=[
            const((n, heads)),
            const((n, heads)),
            const((16, inner)),
            pl.BlockSpec((step // 2, n), lambda i: (i, 0)),
            pl.BlockSpec((step // 2, n), lambda i: (i, 0)),
            pl.BlockSpec((n, step // 2), lambda i: (0, i)),
            pl.BlockSpec((n, step // 2), lambda i: (0, i)),
        ],
        out_shape=[
            near((n, heads), f32),
            near((n, heads), f32),
            near((16, inner), f32),
            near((width // 2, n)),
            kept((width // 2, n)),
            kept((n, width // 2)),
            kept((n, width // 2)),
        ],
        compiler_params=params(24 if half > 512 else 12),
        cost_estimate=cost(1e8, 8e6),
        name="decay",
    )(on, decay, tokens)


def partial_kernel(tok_ref, weight_ref, out_ref):
    part = dot(tok_ref[...], weight_ref[...])

    @pl.when(pl.program_id(0) == 0)
    def _():
        out_ref[...] = part

    @pl.when(pl.program_id(0) > 0)
    def _():
        out_ref[...] += part


def partial_call(tokens, weight):
    n, width = tokens.shape
    cols = weight.shape[1]
    step = 1024
    return pl.pallas_call(
        partial_kernel,
        grid=(width // step,),
        in_specs=[
            pl.BlockSpec((n, step), lambda i: (0, i)),
            pl.BlockSpec((step, cols), lambda i: (i, 0)),
        ],
        out_specs=const((n, cols)),
        out_shape=jax.ShapeDtypeStruct((n, cols), f32),
        compiler_params=params(10),
        cost_estimate=cost(8e8, 4e6),
        name="project_own",
    )(in_hbm(tokens), weight)


def project_kernel(
    tok_ref, weight_ref, part_ref, bias_ref, b_ref,
    lhsy_ref, lhsu_ref, wt_ref, rt_ref, w_ref, r_ref, bs_ref, rho_ref, sc_ref, acc_ref,
):
    i = pl.program_id(0)
    part = dot(tok_ref[...], weight_ref[...])

    @pl.when(i == 0)
    def _():
        acc_ref[...] = part_ref[...] + part

    @pl.when(i > 0)
    def _():
        acc_ref[...] += part

    @pl.when(i == pl.num_programs(0) - 1)
    def _():
        projected = acc_ref[...]
        pre = projected[:, 256:384] + bias_ref[...]
        small = jnp.exp(-jnp.abs(pre))
        step = jnp.maximum(pre, 0.0) + jnp.log1p(small)
        sig = jnp.where(pre >= 0, 1.0, small) / (1.0 + small)
        rho_ref[...] = jnp.where(pre < -15.0, 1.0, sig / jnp.maximum(step, 1e-8))
        bs_ref[...] = step * b_ref[...]
        write = projected[:, :128].astype(bf16)
        read = projected[:, 128:256].astype(bf16)
        w_ref[...] = write
        r_ref[...] = read
        causal = lax.broadcasted_iota(jnp.int32, (CHUNK, CHUNK), 0) >= lax.broadcasted_iota(
            jnp.int32, (CHUNK, CHUNK), 1
        )
        for k, rows in chunks():
            wf, rf = write[rows].astype(f32), read[rows].astype(f32)
            scores = jnp.where(causal, dot_nt(read[rows], write[rows]), 0.0)
            most = jnp.max(jnp.max(jnp.abs(scores), axis=1, keepdims=True), axis=0, keepdims=True)
            power = jnp.exp2(jnp.ceil(jnp.log2(jnp.maximum(most, 1.0))))
            down = 1.0 / power
            lhsy_ref[k] = jnp.concatenate([scores * down, rf * down], axis=1).astype(bf16)
            lhsu_ref[k] = jnp.concatenate([scores.T * down, wf * down], axis=1).astype(bf16)
            wt_ref[k] = wf.T.astype(bf16)
            rt_ref[k] = rf.T.astype(bf16)
            sc_ref[k] = jnp.broadcast_to(power, (8, 128))


def project_call(tokens, weight, part, bias, b):
    n, width = tokens.shape
    cols = weight.shape[1]
    step = 1024
    heads = b.shape[1]
    sds = jax.ShapeDtypeStruct
    shapes = [
        sds((2, CHUNK, 256), bf16),
        sds((2, CHUNK, 256), bf16),
        sds((2, 128, CHUNK), bf16),
        sds((2, 128, CHUNK), bf16),
        sds((n, 128), bf16),
        sds((n, 128), bf16),
        sds((n, heads), f32),
        sds((n, heads), f32),
        sds((2, 8, 128), f32),
    ]
    return pl.pallas_call(
        project_kernel,
        grid=(width // step,),
        in_specs=[
            pl.BlockSpec((n, step), lambda i: (0, i)),
            pl.BlockSpec((step, cols), lambda i: (i, 0)),
            const((n, cols)),
            const((1, heads)),
            const((n, heads)),
        ],
        out_specs=[const(x.shape) for x in shapes],
        out_shape=shapes,
        scratch_shapes=[pltpu.VMEM((n, cols), f32)],
        compiler_params=params(12),
        cost_estimate=cost(8e8, 4e6),
        name="project",
    )(in_hbm(tokens), weight, part, bias, b)


def state_kernel(v_ref, bs_ref, row_ref, wt_ref, x_ref, out_ref, first_ref):
    def tile(i):
        for at, head, _ in subs(i, WIDE):
            rf = row_ref[:, at]
            local = []
            for k, rows in chunks():
                x = (v_ref[rows, at].astype(f32) * spread(bs_ref[rows, :], head)).astype(bf16)
                x_ref[rows, at] = x
                local.append(dot(wt_ref[k], x) * rf[RE1 + k : RE1 + k + 1])
            first_ref[:, at] = local[0].astype(bf16)
            out_ref[:, at] = (rf[EC2 : EC2 + 1] * local[0] + local[1]).astype(bf16)

    each_tile(v_ref.shape[1], tile, WIDE)


def state_call(values, bs, table, wt):
    n, inner = values.shape
    return pl.pallas_call(
        state_kernel,
        in_specs=whole(4),
        out_specs=whole(3),
        out_shape=[near((n, inner)), near((128, inner)), near((128, inner))],
        compiler_params=loop_params(8),
        cost_estimate=cost(2e9, 1.3e7),
        name="states",
    )(on_chip(values), bs, table, wt)


def entering_states(rf, state_ref, first_ref, at):
    state = state_ref[:, at].astype(f32)
    second = rf[IEC1 : IEC1 + 1] * state + first_ref[:, at].astype(f32)
    return (
        (rf[IRS1 : IRS1 + 1] * state).astype(bf16),
        (rf[RS2 : RS2 + 1] * second).astype(bf16),
    )


def outputs_kernel(
    v_ref, o_ref, x_ref, state_ref, first_ref, a_ref, row_ref, lhsy_ref, rt_ref, sc_ref,
    skip_ref, gain_ref, gather_ref,
    out_ref, ga_ref, sgin_ref, sg2_ref, stats_ref,
    pre_ref, ys_ref, square_ref, inner_ref, half_ref, sem_ref,
):
    channels = v_ref.shape[1]
    rows_ref, inv_ref, coef_ref = (stats_ref.at[k] for k in range(3))
    square_ref[...] = jnp.zeros_like(square_ref)
    inner_ref[...] = jnp.zeros_like(inner_ref)
    rows_ref[...] = jnp.zeros_like(rows_ref)

    def forward(i):
        for at, head, _ in subs(i):
            entering = entering_states(row_ref[:, at], state_ref, first_ref, at)
            skip, gain = skip_ref[:, at], gain_ref[:, at]
            for k, rows in chunks():
                y = dot(lhsy_ref[k], jnp.concatenate([x_ref[rows, at], entering[k]], axis=0))
                ys_ref[rows, at] = y
                scale = sc_ref[k, 0:1, 0:1]
                for p, r in blocks(k):
                    pre = spread(a_ref[r, :], head) * y[p] * scale
                    pre += skip * v_ref[r, at].astype(f32)
                    pre_ref[r, at] = pre
                    square = pre * pre
                    both = o_ref[r, at].astype(f32) * gain * pre
                    square_ref[r, :] += square[:, :128] + square[:, 128:]
                    inner_ref[r, :] += both[:, :128] + both[:, 128:]
        sending(pre_ref, out_ref, sem_ref, i).start()

    each_tile(channels, forward)
    mean = jnp.sum(square_ref[...], axis=1, keepdims=True) / channels
    inv = lax.rsqrt(mean + epsilon)
    inner = jnp.sum(inner_ref[...], axis=1, keepdims=True) / channels
    inv_ref[...] = jnp.broadcast_to(inv, inv_ref.shape)
    coef_ref[...] = jnp.broadcast_to(inv * inv * inv * inner, coef_ref.shape)

    def gradient(i):
        sums = jnp.zeros((2 * CHUNK, 128), f32)
        for at, head, place in subs(i):
            rf = row_ref[:, at]
            gain = gain_ref[:, at]
            half = half_ref.at[:, :, place]
            grads = []
            for k, rows in chunks():
                for _, r in blocks(k):
                    g = grad_pre(o_ref, pre_ref, inv_ref, coef_ref, gain, r, at)
                    ga = (spread(a_ref[r, :], head) * g).astype(bf16)
                    ga_ref[r, at] = ga
                    half[0, r, :], half[1, r, :] = split(ga.astype(f32) * ys_ref[r, at])
                grads.append(dot(rt_ref[k], ga_ref[rows, at]) * rf[RS1 + k : RS1 + k + 1])
            sums += collect(half[...], gather_ref[place, :])
            sg2_ref[:, at] = grads[1].astype(bf16)
            sgin_ref[:, at] = (grads[0] + rf[EC1 : EC1 + 1] * grads[1]).astype(bf16)
        back = pltpu.roll(sums, TILE // 64 * i, 1)
        for k, rows in chunks():
            rows_ref[rows, :] += back[rows] * sc_ref[k, 0:1, 0:1]

    each_tile(channels, gradient)
    for i in range(channels // TILE):
        sending(pre_ref, out_ref, sem_ref, i).wait()


def grad_pre(o_ref, pre_ref, inv_ref, coef_ref, gain, r, at):
    inv = jnp.concatenate([inv_ref[r, :]] * 2, axis=1)
    coef = jnp.concatenate([coef_ref[r, :]] * 2, axis=1)
    return inv * (o_ref[r, at].astype(f32) * gain) - pre_ref[r, at] * coef


def outputs_call(
    values, out_grad, x, state, first, a, table, lhsy, rt, sc, skip, gain, gather
):
    n, inner = values.shape
    return pl.pallas_call(
        outputs_kernel,
        in_specs=whole(13),
        out_specs=[pl.BlockSpec(memory_space=pltpu.HBM), *whole(4)],
        out_shape=[
            pltpu.HBM((n, inner), f32),
            near((n, inner)),
            near((128, inner)),
            near((128, inner)),
            near((3, n, 128), f32),
        ],
        scratch_shapes=[
            pltpu.VMEM((n, inner), f32),
            pltpu.VMEM((n, inner), f32),
            pltpu.VMEM((n, 128), f32),
            pltpu.VMEM((n, 128), f32),
            pltpu.VMEM((2, n, TILE), bf16),
            pltpu.SemaphoreType.DMA((inner // TILE,)),
        ],
        compiler_params=loop_params(24),
        cost_estimate=cost(6e9, 4e7),
        name="outputs",
    )(on_chip(values), on_chip(out_grad), on_chip(x), on_chip(state), on_chip(first), a, table, lhsy, rt, sc, skip, gain, gather)


def read_kernel(ga_ref, x_ref, state_ref, first_ref, row_ref, out_ref):
    out_ref[...] = jnp.zeros_like(out_ref)

    def tile(i):
        sums = [jnp.zeros((CHUNK, 256), f32) for _ in range(2)]
        for at, _, _ in subs(i, WIDE):
            rf = row_ref[:, at]
            entering = entering_states(rf, state_ref, first_ref, at)
            for k, rows in chunks():
                right = jnp.concatenate([x_ref[rows, at], entering[k]], axis=0)
                sums[k] += dot_nt(ga_ref[rows, at], right)
        for k in range(2):
            out_ref[k] += sums[k]

    each_tile(ga_ref.shape[1], tile, WIDE)


def read_call(ga, x, state, first, table):
    return pl.pallas_call(
        read_kernel,
        in_specs=whole(5),
        out_specs=whole(1)[0],
        out_shape=near((2, CHUNK, 256), f32),
        compiler_params=loop_params(8),
        cost_estimate=cost(1.2e9, 1.2e7),
        name="read_grads",
    )(on_chip(ga), on_chip(x), on_chip(state), on_chip(first), table)


def leaving_states(rf, later, sg2_ref, at):
    middle = sg2_ref[:, at].astype(f32) + rf[LEC2 : LEC2 + 1] * later
    return [
        (rf[RE1 : RE1 + 1] * middle).astype(bf16),
        (rf[LRE2 : LRE2 + 1] * later).astype(bf16),
    ]


def backward_kernel(
    ga_ref, x_ref, later_ref, sg2_ref, sout_ref, row_ref, lhsu_ref, sc_ref,
    gather_ref, gsr_ref, w_ref, r_ref, rho_ref,
    gp_ref, sums_ref,
    gw_ref, half_ref,
):
    n = ga_ref.shape[0]
    cols_ref, end_ref = sums_ref.at[:n], sums_ref.at[n:]
    sums_ref[...] = jnp.zeros_like(sums_ref)
    gw_ref[...] = jnp.zeros_like(gw_ref)

    def tile(i):
        sums = jnp.zeros((n + 16, 128), f32)
        writes = jnp.zeros((n, 256), f32)
        for at, _, place in subs(i, WIDE):
            half = half_ref.at[:, :, place]
            rf = row_ref[:, at]
            later = later_ref[:, at].astype(f32)
            leaving = leaving_states(rf, later, sg2_ref, at)
            both = later * sout_ref[:, at].astype(f32) * rf[LON : LON + 1]
            half[0, n:, :], half[1, n:, :] = split(jnp.sum(both.reshape(8, 16, SUB), axis=0))
            for k, rows in chunks():
                u = dot(lhsu_ref[k], jnp.concatenate([ga_ref[rows, at], leaving[k]], axis=0))
                for p, r in blocks(k):
                    half[0, r, :], half[1, r, :] = split(x_ref[r, at].astype(f32) * u[p])
            writes += dot_nt(x_ref[:, at], jnp.concatenate(leaving, axis=0))
            sums += collect(half[...], gather_ref[place, :])
        back = pltpu.roll(sums, WIDE // 64 * i, 1)
        for k, rows in chunks():
            cols_ref[rows, :] += back[rows] * sc_ref[k, 0:1, 0:1]
            gw_ref[rows, :] += writes[rows, 128 * k : 128 * k + 128]
        end_ref[...] += back[n:]

    each_tile(ga_ref.shape[1], tile, WIDE)
    causal = lax.broadcasted_iota(jnp.int32, (CHUNK, CHUNK), 0) >= lax.broadcasted_iota(
        jnp.int32, (CHUNK, CHUNK), 1
    )
    for k, rows in chunks():
        scores = jnp.where(causal, gsr_ref[k, :, :128], 0.0)
        read = gsr_ref[k, :, 128:] + dot(scores.astype(bf16), w_ref[rows, :])
        write = gw_ref[rows, :] + dot(scores.T.astype(bf16), r_ref[rows, :])
        gp_ref[rows, 0:128] = write.astype(bf16)
        gp_ref[rows, 128:256] = read.astype(bf16)
    gp_ref[:, 256:384] = (cols_ref[...] * rho_ref[...]).astype(bf16)


def backward_call(ga, x, later, sg2, sout, table, lhsu, sc, gather, gsr, w, r, rho):
    n, inner = ga.shape
    return pl.pallas_call(
        backward_kernel,
        in_specs=whole(13),
        out_specs=whole(2),
        out_shape=[near((n, 384)), near((n + 16, 128), f32)],
        scratch_shapes=[pltpu.VMEM((n, 128), f32), pltpu.VMEM((2, n + 16, WIDE), bf16)],
        compiler_params=loop_params(14),
        cost_estimate=cost(4e9, 2.5e7),
        name="backward",
    )(on_chip(ga), on_chip(x), on_chip(later), on_chip(sg2), on_chip(sout), table, lhsu, sc, gather, gsr, w, r, rho)


def finish_kernel(
    o_ref, pre_ref, ga_ref, later_ref, sg2_ref, row_ref, skip_ref, gain_ref,
    lhsu_ref, bs_ref, sc_ref, stats_ref, sums_ref,
    mixed_ref, vg_ref, gd_ref,
):
    i = pl.program_id(0)
    rows_ref, inv_ref, coef_ref = (stats_ref.at[k] for k in range(3))
    for j in range(LAST // SUB):
        at = slice(j * SUB, (j + 1) * SUB)
        head = (LAST * i + j * SUB) // 64
        leaving = leaving_states(row_ref[:, at], later_ref[:, at].astype(f32), sg2_ref, at)
        skip, gain = skip_ref[:, at], gain_ref[:, at]
        for k, rows in chunks():
            u = dot(lhsu_ref[k], jnp.concatenate([ga_ref[rows, at], leaving[k]], axis=0))
            scale = sc_ref[k, 0:1, 0:1]
            for p, r in blocks(k):
                inv = jnp.concatenate([inv_ref[r, :]] * 2, axis=1)
                mixed_ref[r, at] = (pre_ref[r, at] * inv * gain).astype(bf16)
                g = grad_pre(o_ref, pre_ref, inv_ref, coef_ref, gain, r, at)
                vg = spread(bs_ref[r, :], head) * u[p] * scale + skip * g
                vg_ref[r, at] = vg.astype(bf16)

    @pl.when(i == pl.num_programs(0) - 1)
    def _():
        n = rows_ref.shape[0]
        upper = lax.broadcasted_iota(jnp.int32, (n, n), 0) <= lax.broadcasted_iota(
            jnp.int32, (n, n), 1
        )
        change = rows_ref[...] - sums_ref[:n, :]
        total = dot_exact(jnp.where(upper, 1.0, 0.0).astype(f32), change)
        gd_ref[...] = total + jnp.sum(sums_ref[n:, :], axis=0, keepdims=True)


def finish_call(
    out_grad, pre, ga, later, sg2, table, skip, gain, lhsu, bs, sc, stats, sums
):
    n, inner = ga.shape

    def tiled(rows):
        return pl.BlockSpec((rows, LAST), lambda i: (0, i))

    return pl.pallas_call(
        finish_kernel,
        grid=(inner // LAST,),
        in_specs=[
            tiled(n),
            tiled(n),
            tiled(n),
            tiled(128),
            tiled(128),
            tiled(16),
            tiled(1),
            tiled(1),
            const(lhsu.shape),
            const(bs.shape),
            const(sc.shape),
            const(stats.shape),
            const(sums.shape),
        ],
        out_specs=[tiled(n), tiled(n), const((n, 128))],
        out_shape=[kept((n, inner)), kept((n, inner)), jax.ShapeDtypeStruct((n, 128), f32)],
        compiler_params=params(14),
        cost_estimate=cost(3e9, 2e7),
        name="finish",
    )(in_hbm(out_grad), in_hbm(pre), ga, later, sg2, table, skip, gain, lhsu, bs, sc, stats, sums)


def term_kernel(tok_ref, gp_ref, out_ref):
    for start in range(0, tok_ref.shape[0], 256):
        at = slice(start, start + 256)
        out_ref[at, :] = dot(tok_ref[at, :], gp_ref[...])


def term_call(tok, gp):
    return pl.pallas_call(
        term_kernel,
        in_specs=whole(2),
        out_specs=whole(1)[0],
        out_shape=near((tok.shape[0], gp.shape[1]), f32),
        compiler_params=loop_params(4),
        cost_estimate=cost(8e8, 3e6),
        name="term_own",
    )(tok, gp)


def both_kernel(tok_ref, gp_ref, own_ref, out_ref):
    for start in range(0, tok_ref.shape[0], 256):
        at = slice(start, start + 256)
        out_ref[at, :] = (own_ref[at, :] + dot(tok_ref[at, :], gp_ref[...])).astype(bf16)


def both_call(tok, gp, own):
    return pl.pallas_call(
        both_kernel,
        in_specs=whole(3),
        out_specs=whole(1)[0],
        out_shape=jax.ShapeDtypeStruct(own.shape, bf16),
        compiler_params=loop_params(8),
        cost_estimate=cost(8e8, 3e6),
        name="term_both",
    )(on_chip(tok), gp, own)


def total_kernel(parts_ref, out_ref):
    sums = [parts_ref[k].astype(f32) for k in range(parts_ref.shape[0])]
    while len(sums) > 1:
        sums = [sum(sums[k : k + 2]) for k in range(0, len(sums), 2)]
    out_ref[...] = sums[0]


def total_call(parts):
    return pl.pallas_call(
        total_kernel,
        in_specs=whole(1),
        out_specs=whole(1)[0],
        out_shape=near(parts.shape[1:], f32),
        compiler_params=loop_params(4),
        name="total",
    )(on_chip(parts))


SWAP = [(0, 1), (1, 0)]


def on_device(tokens, values, log_decay, out_grad, proj_weight, dt_bias, skip, gain):
    tokens, values, log_decay, out_grad = tokens[0], values[0], log_decay[0], out_grad[0]
    me = lax.axis_index("ctx")
    owners = lax.axis_size("dp")
    n, inner = values.shape
    heads = log_decay.shape[1]
    half = proj_weight.shape[0] // 2
    cols = proj_weight.shape[1]

    mine = lax.dynamic_slice_in_dim(proj_weight, me * half, half, 0)
    own = lax.all_to_all(
        jnp.broadcast_to(mine[None], (owners, half, cols)), "dp", 0, 0, tiled=True
    ).reshape(owners * half, cols)

    late = me.astype(f32).reshape(1)
    a, b, table, keep, give, tok_own, tok_other = decay_call(
        late, log_decay, tokens, half, inner
    )
    lane_head = jnp.arange(WIDE) // (inner // heads)
    gather = (lane_head[:, None] == jnp.arange(128)[None, :]).astype(bf16)
    skip_row = jnp.repeat(skip, inner // heads)[None]
    own, a, b, table, keep, give, tok_own, tok_other, gather, skip_row = lax.optimization_barrier(
        (own, a, b, table, keep, give, tok_own, tok_other, gather, skip_row)
    )
    other = lax.ppermute(own, "ctx", SWAP)
    part = partial_call(tok_own, own)
    lhsy, lhsu, wt, rt, w, r, bs, rho, sc = project_call(tok_other, other, part, dt_bias[None], b)
    x, sout, first = state_call(values, bs, table, wt)
    state = lax.ppermute(sout, "ctx", SWAP)
    got = lax.ppermute(give, "ctx", SWAP)
    pre, ga, sgin, sg2, stats = outputs_call(
        values, out_grad, x, state, first, a, table, lhsy, rt, sc, skip_row, gain[None], gather
    )
    later = lax.ppermute(sgin, "ctx", SWAP)
    gsr = read_call(ga, x, state, first, table)
    gp, sums = backward_call(
        ga, x, later, sg2, sout, table, lhsu, sc, gather, gsr, w, r, rho
    )
    gp_other = lax.ppermute(gp, "ctx", SWAP)
    term = both_call(got, gp_other, term_call(keep, gp))
    parts = lax.all_to_all(term.reshape(owners, half, cols), "dp", 0, 0, tiled=True)
    mixed, grad_values, grad_decay = finish_call(
        out_grad, pre, ga, later, sg2, table, skip_row, gain[None], lhsu, bs, sc, stats, sums
    )
    lead = jnp.where(me == 0, own, other).reshape(owners, half, cols)
    trail = jnp.where(me == 0, other, own).reshape(owners, half, cols)
    weight = jnp.concatenate([lead, trail], axis=1).reshape(2 * owners * half, cols)
    grad_tokens = dot_nt(gp, weight).astype(bf16)
    parts, grad_tokens, mixed, grad_values, grad_decay = lax.optimization_barrier(
        (parts, grad_tokens, mixed, grad_values, grad_decay)
    )
    owned = total_call(parts)
    owned_other = lax.ppermute(owned, "ctx", SWAP)
    grad_weight = jnp.where(
        me == 0,
        jnp.concatenate([owned, owned_other], axis=0),
        jnp.concatenate([owned_other, owned], axis=0),
    )
    return mixed[None], grad_tokens[None], grad_values[None], grad_decay[None], grad_weight


def solution(mesh):
    rows = P("dp", "ctx", None)
    return jax.shard_map(
        on_device,
        mesh=mesh,
        in_specs=(rows, rows, rows, rows, P("dp", None), P(), P(), P()),
        out_specs=(rows, rows, rows, rows, P("dp", None)),
        check_vma=False,
    )
```

```python
import functools

import jax
import jax.numpy as jnp
from jax import lax
from jax.experimental import pallas as pl
from jax.experimental.pallas import tpu as pltpu
from jax.sharding import PartitionSpec as P

epsilon = 1e-05
bf16, f32 = jnp.bfloat16, jnp.float32
CHUNK = 128
TILE = 2048
WIDE = 4096
SUB = 256
BLOCK = 32
LAST = 1024
RS1, RS2, RE1, RE2, EC1, EC2, IRS1, IEC1, LRE2, LEC2, LON = range(11)


def dot(a, b):
    return jnp.dot(a, b, preferred_element_type=f32)


def dot_nt(a, b):
    return lax.dot_general(a, b, (((1,), (1,)), ((), ())), preferred_element_type=f32)


def dot_exact(a, b):
    return lax.dot_general(
        a, b, (((1,), (0,)), ((), ())), precision=lax.Precision.HIGHEST, preferred_element_type=f32
    )


def split(x):
    high = x.astype(bf16)
    return high, (x - high.astype(f32)).astype(bf16)


def spread(x, head):
    which = lax.shift_right_logical(lax.broadcasted_iota(jnp.int32, x.shape, 1), 6) + head
    parts = [
        jnp.take_along_axis(x, which + 2 * q, axis=1, mode="promise_in_bounds") for q in range(2)
    ]
    return jnp.concatenate(parts, axis=1)


def collect(halves, gather):
    rows = halves.shape[1]
    total = dot(halves.reshape(2 * rows, SUB), gather)
    return total[:rows] + total[rows:]


def chunks():
    return [(k, slice(k * CHUNK, (k + 1) * CHUNK)) for k in range(2)]


def subs(i, tile=TILE):
    return [
        (
            pl.ds(pl.multiple_of(i * tile + j * SUB, SUB), SUB),
            (tile * i + j * SUB) // 64,
            slice(j * SUB, (j + 1) * SUB),
        )
        for j in range(tile // SUB)
    ]


def each_tile(width, body, tile=TILE):
    def step(i, unused):
        body(i)
        return unused

    lax.fori_loop(0, width // tile, step, 0)


def blocks(k):
    return [
        (slice(r, r + BLOCK), slice(k * CHUNK + r, k * CHUNK + r + BLOCK))
        for r in range(0, CHUNK, BLOCK)
    ]


def params(limit):
    return pltpu.CompilerParams(
        dimension_semantics=("arbitrary",), vmem_limit_bytes=limit * 2**20
    )


def near(shape, dtype=bf16):
    return pltpu.VMEM(shape, dtype)


def kept(shape):
    return pltpu.HBM(shape, bf16)


def on_chip(x):
    return pltpu.with_memory_space_constraint(x, pltpu.VMEM)


def in_hbm(x):
    return pltpu.with_memory_space_constraint(x, pltpu.HBM)


def whole(count):
    return [pl.BlockSpec(memory_space=pltpu.VMEM)] * count


def sending(source, out, sem, i):
    place = pl.ds(pl.multiple_of(i * TILE, TILE), TILE)
    return pltpu.make_async_copy(source.at[:, place], out.at[:, place], sem.at[i])


def loop_params(limit):
    return pltpu.CompilerParams(vmem_limit_bytes=limit * 2**20)


def cost(flops, moved):
    return pl.CostEstimate(flops=int(flops), bytes_accessed=int(moved), transcendentals=0)


def const(shape):
    return pl.BlockSpec(shape, lambda i: (0,) * len(shape))


def decay_kernel(half, on_ref, decay_ref, tok_ref, a_ref, b_ref, row_ref, keep_ref, give_ref, own_ref, other_ref):
    late = on_ref[0]
    turned = tok_ref[...].T
    groups = turned.shape[0] // (2 * half)
    turned = turned.reshape(groups, 2, half, turned.shape[1])
    flat = (groups * half, turned.shape[3])
    lead, trail = turned[:, 0].reshape(flat), turned[:, 1].reshape(flat)
    keep = jnp.where(late > 0.5, trail, lead)
    give = jnp.where(late > 0.5, lead, trail)
    keep_ref[...] = keep
    give_ref[...] = give
    own_ref[...] = keep.T
    other_ref[...] = give.T

    @pl.when(pl.program_id(0) == 0)
    def _():
        n = decay_ref.shape[0]
        lower = lax.broadcasted_iota(jnp.int32, (n, n), 0) >= lax.broadcasted_iota(
            jnp.int32, (n, n), 1
        )
        total = dot_exact(jnp.where(lower, 1.0, 0.0).astype(f32), decay_ref[...])
        middle = [total[k * CHUNK + CHUNK // 2 - 1 :][:1] for k in range(2)]
        end = [total[(k + 1) * CHUNK - 1 :][:1] for k in range(2)]
        for k, rows in chunks():
            a_ref[rows, :] = jnp.exp(total[rows] - middle[k])
            b_ref[rows, :] = jnp.exp(middle[k] - total[rows])
        early = 1.0 - late
        rs1, rs2 = jnp.exp(middle[0]), jnp.exp(middle[1] - end[0])
        re1, re2 = jnp.exp(end[0] - middle[0]), jnp.exp(end[1] - middle[1])
        ec1, ec2 = jnp.exp(end[0]), jnp.exp(end[1] - end[0])
        table = [rs1, rs2, re1, re2, ec1, ec2, rs1 * late, ec1 * late, re2 * early, ec2 * early]
        table.append(jnp.ones_like(rs1) * early)
        table += [jnp.zeros_like(rs1)] * (16 - len(table))
        table = jnp.concatenate(table, axis=0)
        for head in range(0, table.shape[1], SUB // 64):
            row_ref[:, head * 64 : head * 64 + SUB] = spread(table, head)


def decay_call(on, decay, tokens, half, inner):
    n, heads = decay.shape
    width = tokens.shape[1]
    step = max(1024, 2 * half)
    sds = jax.ShapeDtypeStruct
    return pl.pallas_call(
        functools.partial(decay_kernel, half),
        grid=(width // step,),
        in_specs=[
            pl.BlockSpec(memory_space=pltpu.SMEM),
            const((n, heads)),
            pl.BlockSpec((n, step), lambda i: (0, i)),
        ],
        out_specs=[
            const((n, heads)),
            const((n, heads)),
            const((16, inner)),
            pl.BlockSpec((step // 2, n), lambda i: (i, 0)),
            pl.BlockSpec((step // 2, n), lambda i: (i, 0)),
            pl.BlockSpec((n, step // 2), lambda i: (0, i)),
            pl.BlockSpec((n, step // 2), lambda i: (0, i)),
        ],
        out_shape=[
            near((n, heads), f32),
            near((n, heads), f32),
            near((16, inner), f32),
            near((width // 2, n)),
            kept((width // 2, n)),
            near((n, width // 2)),
            near((n, width // 2)),
        ],
        compiler_params=params(24 if half > 512 else 12),
        cost_estimate=cost(1e8, 8e6),
        name="decay",
    )(on, decay, tokens)


def partial_kernel(tok_ref, weight_ref, out_ref):
    part = dot(tok_ref[...], weight_ref[...])

    @pl.when(pl.program_id(0) == 0)
    def _():
        out_ref[...] = part

    @pl.when(pl.program_id(0) > 0)
    def _():
        out_ref[...] += part


def partial_call(tokens, weight):
    n, width = tokens.shape
    cols = weight.shape[1]
    step = 1024
    return pl.pallas_call(
        partial_kernel,
        grid=(width // step,),
        in_specs=[
            pl.BlockSpec((n, step), lambda i: (0, i)),
            pl.BlockSpec((step, cols), lambda i: (i, 0)),
        ],
        out_specs=const((n, cols)),
        out_shape=jax.ShapeDtypeStruct((n, cols), f32),
        compiler_params=params(10),
        cost_estimate=cost(8e8, 4e6),
        name="project_own",
    )(tokens, weight)


def project_kernel(
    tok_ref, weight_ref, part_ref, bias_ref, b_ref,
    lhsy_ref, lhsu_ref, wt_ref, rt_ref, w_ref, r_ref, bs_ref, rho_ref, sc_ref, acc_ref,
):
    i = pl.program_id(0)
    part = dot(tok_ref[...], weight_ref[...])

    @pl.when(i == 0)
    def _():
        acc_ref[...] = part_ref[...] + part

    @pl.when(i > 0)
    def _():
        acc_ref[...] += part

    @pl.when(i == pl.num_programs(0) - 1)
    def _():
        projected = acc_ref[...]
        pre = projected[:, 256:384] + bias_ref[...]
        small = jnp.exp(-jnp.abs(pre))
        step = jnp.maximum(pre, 0.0) + jnp.log1p(small)
        sig = jnp.where(pre >= 0, 1.0, small) / (1.0 + small)
        rho_ref[...] = jnp.where(pre < -15.0, 1.0, sig / jnp.maximum(step, 1e-8))
        bs_ref[...] = step * b_ref[...]
        write = projected[:, :128].astype(bf16)
        read = projected[:, 128:256].astype(bf16)
        w_ref[...] = write
        r_ref[...] = read
        causal = lax.broadcasted_iota(jnp.int32, (CHUNK, CHUNK), 0) >= lax.broadcasted_iota(
            jnp.int32, (CHUNK, CHUNK), 1
        )
        for k, rows in chunks():
            wf, rf = write[rows].astype(f32), read[rows].astype(f32)
            scores = jnp.where(causal, dot_nt(read[rows], write[rows]), 0.0)
            most = jnp.max(jnp.max(jnp.abs(scores), axis=1, keepdims=True), axis=0, keepdims=True)
            power = jnp.exp2(jnp.ceil(jnp.log2(jnp.maximum(most, 1.0))))
            down = 1.0 / power
            lhsy_ref[k] = jnp.concatenate([scores * down, rf * down], axis=1).astype(bf16)
            lhsu_ref[k] = jnp.concatenate([scores.T * down, wf * down], axis=1).astype(bf16)
            wt_ref[k] = wf.T.astype(bf16)
            rt_ref[k] = rf.T.astype(bf16)
            sc_ref[k] = jnp.broadcast_to(power, (8, 128))


def project_call(tokens, weight, part, bias, b):
    n, width = tokens.shape
    cols = weight.shape[1]
    step = 1024
    heads = b.shape[1]
    sds = jax.ShapeDtypeStruct
    shapes = [
        sds((2, CHUNK, 256), bf16),
        sds((2, CHUNK, 256), bf16),
        sds((2, 128, CHUNK), bf16),
        sds((2, 128, CHUNK), bf16),
        sds((n, 128), bf16),
        sds((n, 128), bf16),
        sds((n, heads), f32),
        sds((n, heads), f32),
        sds((2, 8, 128), f32),
    ]
    return pl.pallas_call(
        project_kernel,
        grid=(width // step,),
        in_specs=[
            pl.BlockSpec((n, step), lambda i: (0, i)),
            pl.BlockSpec((step, cols), lambda i: (i, 0)),
            const((n, cols)),
            const((1, heads)),
            const((n, heads)),
        ],
        out_specs=[const(x.shape) for x in shapes],
        out_shape=shapes,
        scratch_shapes=[pltpu.VMEM((n, cols), f32)],
        compiler_params=params(12),
        cost_estimate=cost(8e8, 4e6),
        name="project",
    )(tokens, weight, part, bias, b)


def state_kernel(v_ref, bs_ref, row_ref, wt_ref, x_ref, out_ref, first_ref):
    def tile(i):
        for at, head, _ in subs(i, WIDE):
            rf = row_ref[:, at]
            local = []
            for k, rows in chunks():
                x = (v_ref[rows, at].astype(f32) * spread(bs_ref[rows, :], head)).astype(bf16)
                x_ref[rows, at] = x
                local.append(dot(wt_ref[k], x) * rf[RE1 + k : RE1 + k + 1])
            first_ref[:, at] = local[0].astype(bf16)
            out_ref[:, at] = (rf[EC2 : EC2 + 1] * local[0] + local[1]).astype(bf16)

    each_tile(v_ref.shape[1], tile, WIDE)


def state_call(values, bs, table, wt):
    n, inner = values.shape
    return pl.pallas_call(
        state_kernel,
        in_specs=whole(4),
        out_specs=whole(3),
        out_shape=[near((n, inner)), near((128, inner)), near((128, inner))],
        compiler_params=loop_params(8),
        cost_estimate=cost(2e9, 1.3e7),
        name="states",
    )(on_chip(values), bs, table, wt)


def entering_states(rf, state_ref, first_ref, at):
    state = state_ref[:, at].astype(f32)
    second = rf[IEC1 : IEC1 + 1] * state + first_ref[:, at].astype(f32)
    return (
        (rf[IRS1 : IRS1 + 1] * state).astype(bf16),
        (rf[RS2 : RS2 + 1] * second).astype(bf16),
    )


def outputs_kernel(
    v_ref, o_ref, x_ref, state_ref, first_ref, a_ref, row_ref, lhsy_ref, rt_ref, sc_ref,
    skip_ref, gain_ref, gather_ref,
    out_ref, factors_ref, ga_ref, sgin_ref, sg2_ref, rows_ref,
    pre_ref, ys_ref, square_ref, inner_ref, norm_ref, half_ref, sem_ref,
):
    channels = v_ref.shape[1]
    steps = channels // TILE
    inv_ref, coef_ref = norm_ref.at[0], norm_ref.at[1]
    square_ref[...] = jnp.zeros_like(square_ref)
    inner_ref[...] = jnp.zeros_like(inner_ref)
    rows_ref[...] = jnp.zeros_like(rows_ref)

    def forward(i):
        for at, head, _ in subs(i):
            entering = entering_states(row_ref[:, at], state_ref, first_ref, at)
            skip, gain = skip_ref[:, at], gain_ref[:, at]
            for k, rows in chunks():
                y = dot(lhsy_ref[k], jnp.concatenate([x_ref[rows, at], entering[k]], axis=0))
                ys_ref[rows, at] = y
                scale = sc_ref[k, 0:1, 0:1]
                for p, r in blocks(k):
                    pre = spread(a_ref[r, :], head) * y[p] * scale
                    pre += skip * v_ref[r, at].astype(f32)
                    pre_ref[r, at] = pre
                    square = pre * pre
                    both = o_ref[r, at].astype(f32) * gain * pre
                    square_ref[r, :] += square[:, :128] + square[:, 128:]
                    inner_ref[r, :] += both[:, :128] + both[:, 128:]
        sending(pre_ref, out_ref, sem_ref, i).start()

    each_tile(channels, forward)
    mean = jnp.sum(square_ref[...], axis=1, keepdims=True) / channels
    inv = lax.rsqrt(mean + epsilon)
    inner = jnp.sum(inner_ref[...], axis=1, keepdims=True) / channels
    inv_ref[...] = jnp.broadcast_to(inv, inv_ref.shape)
    coef_ref[...] = jnp.broadcast_to(inv * inv * inv * inner, coef_ref.shape)
    factors = pltpu.make_async_copy(norm_ref, factors_ref, sem_ref.at[steps])
    factors.start()

    def gradient(i):
        sums = jnp.zeros((2 * CHUNK, 128), f32)
        for at, head, place in subs(i):
            rf = row_ref[:, at]
            gain = gain_ref[:, at]
            half = half_ref.at[:, :, place]
            grads = []
            for k, rows in chunks():
                for _, r in blocks(k):
                    g = grad_pre(o_ref, pre_ref, inv_ref, coef_ref, gain, r, at)
                    ga = (spread(a_ref[r, :], head) * g).astype(bf16)
                    ga_ref[r, at] = ga
                    half[0, r, :], half[1, r, :] = split(ga.astype(f32) * ys_ref[r, at])
                grads.append(dot(rt_ref[k], ga_ref[rows, at]) * rf[RS1 + k : RS1 + k + 1])
            sums += collect(half[...], gather_ref[place, :])
            sg2_ref[:, at] = grads[1].astype(bf16)
            sgin_ref[:, at] = (grads[0] + rf[EC1 : EC1 + 1] * grads[1]).astype(bf16)
        back = pltpu.roll(sums, TILE // 64 * i, 1)
        for k, rows in chunks():
            rows_ref[rows, :] += back[rows] * sc_ref[k, 0:1, 0:1]

    each_tile(channels, gradient)
    for i in range(steps):
        sending(pre_ref, out_ref, sem_ref, i).wait()
    factors.wait()


def grad_pre(o_ref, pre_ref, inv_ref, coef_ref, gain, r, at):
    inv = jnp.concatenate([inv_ref[r, :]] * 2, axis=1)
    coef = jnp.concatenate([coef_ref[r, :]] * 2, axis=1)
    return inv * (o_ref[r, at].astype(f32) * gain) - pre_ref[r, at] * coef


def outputs_call(
    values, out_grad, x, state, first, a, table, lhsy, rt, sc, skip, gain, gather
):
    n, inner = values.shape
    return pl.pallas_call(
        outputs_kernel,
        in_specs=whole(13),
        out_specs=[pl.BlockSpec(memory_space=pltpu.HBM)] * 2 + whole(4),
        out_shape=[
            pltpu.HBM((n, inner), f32),
            pltpu.HBM((2, n, 128), f32),
            near((n, inner)),
            near((128, inner)),
            near((128, inner)),
            near((n, 128), f32),
        ],
        scratch_shapes=[
            pltpu.VMEM((n, inner), f32),
            pltpu.VMEM((n, inner), f32),
            pltpu.VMEM((n, 128), f32),
            pltpu.VMEM((n, 128), f32),
            pltpu.VMEM((2, n, 128), f32),
            pltpu.VMEM((2, n, TILE), bf16),
            pltpu.SemaphoreType.DMA((inner // TILE + 1,)),
        ],
        compiler_params=loop_params(24),
        cost_estimate=cost(6e9, 4e7),
        name="outputs",
    )(on_chip(values), on_chip(out_grad), on_chip(x), on_chip(state), on_chip(first), a, table, lhsy, rt, sc, skip, gain, gather)


def read_kernel(ga_ref, x_ref, state_ref, first_ref, row_ref, out_ref):
    out_ref[...] = jnp.zeros_like(out_ref)

    def tile(i):
        sums = [jnp.zeros((CHUNK, 256), f32) for _ in range(2)]
        for at, _, _ in subs(i, WIDE):
            rf = row_ref[:, at]
            entering = entering_states(rf, state_ref, first_ref, at)
            for k, rows in chunks():
                right = jnp.concatenate([x_ref[rows, at], entering[k]], axis=0)
                sums[k] += dot_nt(ga_ref[rows, at], right)
        for k in range(2):
            out_ref[k] += sums[k]

    each_tile(ga_ref.shape[1], tile, WIDE)


def read_call(ga, x, state, first, table):
    return pl.pallas_call(
        read_kernel,
        in_specs=whole(5),
        out_specs=whole(1)[0],
        out_shape=near((2, CHUNK, 256), f32),
        compiler_params=loop_params(8),
        cost_estimate=cost(1.2e9, 1.2e7),
        name="read_grads",
    )(on_chip(ga), on_chip(x), on_chip(state), on_chip(first), table)


def leaving_states(rf, later, sg2_ref, at):
    middle = sg2_ref[:, at].astype(f32) + rf[LEC2 : LEC2 + 1] * later
    return [
        (rf[RE1 : RE1 + 1] * middle).astype(bf16),
        (rf[LRE2 : LRE2 + 1] * later).astype(bf16),
    ]


def backward_kernel(
    ga_ref, x_ref, later_ref, sg2_ref, sout_ref, row_ref, lhsu_ref, sc_ref,
    gather_ref, gsr_ref, w_ref, r_ref, rho_ref, rows_ref,
    gp_ref, sums_ref,
    gw_ref, half_ref,
):
    n = ga_ref.shape[0]
    cols_ref, end_ref = sums_ref.at[:n], sums_ref.at[n:]
    sums_ref[...] = jnp.zeros_like(sums_ref)
    gw_ref[...] = jnp.zeros_like(gw_ref)

    def tile(i):
        sums = jnp.zeros((n + 16, 128), f32)
        writes = jnp.zeros((n, 256), f32)
        for at, _, place in subs(i, WIDE):
            half = half_ref.at[:, :, place]
            rf = row_ref[:, at]
            later = later_ref[:, at].astype(f32)
            leaving = leaving_states(rf, later, sg2_ref, at)
            both = later * sout_ref[:, at].astype(f32) * rf[LON : LON + 1]
            half[0, n:, :], half[1, n:, :] = split(jnp.sum(both.reshape(8, 16, SUB), axis=0))
            for k, rows in chunks():
                u = dot(lhsu_ref[k], jnp.concatenate([ga_ref[rows, at], leaving[k]], axis=0))
                for p, r in blocks(k):
                    half[0, r, :], half[1, r, :] = split(x_ref[r, at].astype(f32) * u[p])
            writes += dot_nt(x_ref[:, at], jnp.concatenate(leaving, axis=0))
            sums += collect(half[...], gather_ref[place, :])
        back = pltpu.roll(sums, WIDE // 64 * i, 1)
        for k, rows in chunks():
            cols_ref[rows, :] += back[rows] * sc_ref[k, 0:1, 0:1]
            gw_ref[rows, :] += writes[rows, 128 * k : 128 * k + 128]
        end_ref[...] += back[n:]

    each_tile(ga_ref.shape[1], tile, WIDE)
    causal = lax.broadcasted_iota(jnp.int32, (CHUNK, CHUNK), 0) >= lax.broadcasted_iota(
        jnp.int32, (CHUNK, CHUNK), 1
    )
    for k, rows in chunks():
        scores = jnp.where(causal, gsr_ref[k, :, :128], 0.0)
        read = gsr_ref[k, :, 128:] + dot(scores.astype(bf16), w_ref[rows, :])
        write = gw_ref[rows, :] + dot(scores.T.astype(bf16), r_ref[rows, :])
        gp_ref[rows, 0:128] = write.astype(bf16)
        gp_ref[rows, 128:256] = read.astype(bf16)
    gp_ref[:, 256:384] = (cols_ref[...] * rho_ref[...]).astype(bf16)
    cols_ref[...] = rows_ref[...] - cols_ref[...]


def backward_call(ga, x, later, sg2, sout, table, lhsu, sc, gather, gsr, w, r, rho, rows):
    n, inner = ga.shape
    return pl.pallas_call(
        backward_kernel,
        in_specs=whole(14),
        out_specs=whole(2),
        out_shape=[near((n, 384)), near((n + 16, 128), f32)],
        scratch_shapes=[pltpu.VMEM((n, 128), f32), pltpu.VMEM((2, n + 16, WIDE), bf16)],
        compiler_params=loop_params(14),
        cost_estimate=cost(4e9, 2.5e7),
        name="backward",
    )(on_chip(ga), on_chip(x), on_chip(later), on_chip(sg2), on_chip(sout), table, lhsu, sc, gather, gsr, w, r, rho, rows)


def finish_kernel(
    o_ref, pre_ref, ga_ref, later_ref, sg2_ref, row_ref, skip_ref, gain_ref,
    lhsu_ref, bs_ref, sc_ref, norm_ref, sums_ref,
    mixed_ref, vg_ref, gd_ref,
):
    i = pl.program_id(0)
    inv_ref, coef_ref = norm_ref.at[0], norm_ref.at[1]
    for j in range(LAST // SUB):
        at = slice(j * SUB, (j + 1) * SUB)
        head = (LAST * i + j * SUB) // 64
        leaving = leaving_states(row_ref[:, at], later_ref[:, at].astype(f32), sg2_ref, at)
        skip, gain = skip_ref[:, at], gain_ref[:, at]
        for k, rows in chunks():
            u = dot(lhsu_ref[k], jnp.concatenate([ga_ref[rows, at], leaving[k]], axis=0))
            scale = sc_ref[k, 0:1, 0:1]
            for p, r in blocks(k):
                inv = jnp.concatenate([inv_ref[r, :]] * 2, axis=1)
                mixed_ref[r, at] = (pre_ref[r, at] * inv * gain).astype(bf16)
                g = grad_pre(o_ref, pre_ref, inv_ref, coef_ref, gain, r, at)
                vg = spread(bs_ref[r, :], head) * u[p] * scale + skip * g
                vg_ref[r, at] = vg.astype(bf16)

    @pl.when(i == pl.num_programs(0) - 1)
    def _():
        n = o_ref.shape[0]
        upper = lax.broadcasted_iota(jnp.int32, (n, n), 0) <= lax.broadcasted_iota(
            jnp.int32, (n, n), 1
        )
        total = dot_exact(jnp.where(upper, 1.0, 0.0).astype(f32), sums_ref[:n, :])
        gd_ref[...] = total + jnp.sum(sums_ref[n:, :], axis=0, keepdims=True)


def finish_call(
    out_grad, pre, ga, later, sg2, table, skip, gain, lhsu, bs, sc, factors, sums
):
    n, inner = ga.shape

    def tiled(rows):
        return pl.BlockSpec((rows, LAST), lambda i: (0, i))

    return pl.pallas_call(
        finish_kernel,
        grid=(inner // LAST,),
        in_specs=[
            tiled(n),
            tiled(n),
            tiled(n),
            tiled(128),
            tiled(128),
            tiled(16),
            tiled(1),
            tiled(1),
            const(lhsu.shape),
            const(bs.shape),
            const(sc.shape),
            const(factors.shape),
            const(sums.shape),
        ],
        out_specs=[tiled(n), tiled(n), const((n, 128))],
        out_shape=[kept((n, inner)), kept((n, inner)), jax.ShapeDtypeStruct((n, 128), f32)],
        compiler_params=params(14),
        cost_estimate=cost(3e9, 2e7),
        name="finish",
    )(in_hbm(out_grad), in_hbm(pre), ga, later, sg2, table, skip, gain, lhsu, bs, sc, factors, sums)


def term_kernel(tok_ref, gp_ref, out_ref):
    for start in range(0, tok_ref.shape[0], 256):
        at = slice(start, start + 256)
        out_ref[at, :] = dot(tok_ref[at, :], gp_ref[...])


def term_call(tok, gp):
    return pl.pallas_call(
        term_kernel,
        in_specs=whole(2),
        out_specs=whole(1)[0],
        out_shape=near((tok.shape[0], gp.shape[1]), f32),
        compiler_params=loop_params(4),
        cost_estimate=cost(8e8, 3e6),
        name="term_own",
    )(tok, gp)


def both_kernel(tok_ref, gp_ref, own_ref, out_ref):
    for start in range(0, tok_ref.shape[0], 256):
        at = slice(start, start + 256)
        out_ref[at, :] = (own_ref[at, :] + dot(tok_ref[at, :], gp_ref[...])).astype(bf16)


def both_call(tok, gp, own):
    return pl.pallas_call(
        both_kernel,
        in_specs=whole(3),
        out_specs=whole(1)[0],
        out_shape=jax.ShapeDtypeStruct(own.shape, bf16),
        compiler_params=loop_params(8),
        cost_estimate=cost(8e8, 3e6),
        name="term_both",
    )(on_chip(tok), gp, own)


def total_kernel(parts_ref, out_ref):
    sums = [parts_ref[k].astype(f32) for k in range(parts_ref.shape[0])]
    while len(sums) > 1:
        sums = [sum(sums[k : k + 2]) for k in range(0, len(sums), 2)]
    out_ref[...] = sums[0]


def total_call(parts):
    return pl.pallas_call(
        total_kernel,
        in_specs=whole(1),
        out_specs=whole(1)[0],
        out_shape=near(parts.shape[1:], f32),
        compiler_params=loop_params(4),
        name="total",
    )(on_chip(parts))


SWAP = [(0, 1), (1, 0)]


def on_device(tokens, values, log_decay, out_grad, proj_weight, dt_bias, skip, gain):
    tokens, values, log_decay, out_grad = tokens[0], values[0], log_decay[0], out_grad[0]
    me = lax.axis_index("ctx")
    owners = lax.axis_size("dp")
    n, inner = values.shape
    heads = log_decay.shape[1]
    half = proj_weight.shape[0] // 2
    cols = proj_weight.shape[1]

    mine = lax.dynamic_slice_in_dim(proj_weight, me * half, half, 0)
    own = lax.all_to_all(
        jnp.broadcast_to(mine[None], (owners, half, cols)), "dp", 0, 0, tiled=True
    ).reshape(owners * half, cols)

    late = me.astype(f32).reshape(1)
    a, b, table, keep, give, tok_own, tok_other = decay_call(
        late, log_decay, tokens, half, inner
    )
    lane_head = jnp.arange(WIDE) // (inner // heads)
    gather = (lane_head[:, None] == jnp.arange(128)[None, :]).astype(bf16)
    skip_row = jnp.repeat(skip, inner // heads)[None]
    own, a, b, table, keep, give, gather, skip_row = lax.optimization_barrier(
        (own, a, b, table, keep, give, gather, skip_row)
    )
    other = lax.ppermute(own, "ctx", SWAP)
    part = partial_call(tok_own, own)
    lhsy, lhsu, wt, rt, w, r, bs, rho, sc = project_call(tok_other, other, part, dt_bias[None], b)
    x, sout, first = state_call(values, bs, table, wt)
    state = lax.ppermute(sout, "ctx", SWAP)
    got = lax.ppermute(give, "ctx", SWAP)
    pre, factors, ga, sgin, sg2, rows = outputs_call(
        values, out_grad, x, state, first, a, table, lhsy, rt, sc, skip_row, gain[None], gather
    )
    later = lax.ppermute(sgin, "ctx", SWAP)
    gsr = read_call(ga, x, state, first, table)
    gp, sums = backward_call(
        ga, x, later, sg2, sout, table, lhsu, sc, gather, gsr, w, r, rho, rows
    )
    gp_other = lax.ppermute(gp, "ctx", SWAP)
    term = both_call(got, gp_other, term_call(keep, gp))
    parts = lax.all_to_all(term.reshape(owners, half, cols), "dp", 0, 0, tiled=True)
    mixed, grad_values, grad_decay = finish_call(
        out_grad, pre, ga, later, sg2, table, skip_row, gain[None], lhsu, bs, sc, factors, sums
    )
    lead = jnp.where(me == 0, own, other).reshape(owners, half, cols)
    trail = jnp.where(me == 0, other, own).reshape(owners, half, cols)
    weight = jnp.concatenate([lead, trail], axis=1).reshape(2 * owners * half, cols)
    grad_tokens = dot_nt(gp, weight).astype(bf16)
    parts, grad_tokens, mixed, grad_values, grad_decay = lax.optimization_barrier(
        (parts, grad_tokens, mixed, grad_values, grad_decay)
    )
    owned = total_call(parts)
    owned_other = lax.ppermute(owned, "ctx", SWAP)
    grad_weight = jnp.where(
        me == 0,
        jnp.concatenate([owned, owned_other], axis=0),
        jnp.concatenate([owned_other, owned], axis=0),
    )
    return mixed[None], grad_tokens[None], grad_values[None], grad_decay[None], grad_weight


def solution(mesh):
    rows = P("dp", "ctx", None)
    return jax.shard_map(
        on_device,
        mesh=mesh,
        in_specs=(rows, rows, rows, rows, P("dp", None), P(), P(), P()),
        out_specs=(rows, rows, rows, rows, P("dp", None)),
        check_vma=False,
    )
```

```python
import functools

import jax
import jax.numpy as jnp
from jax import lax
from jax.experimental import pallas as pl
from jax.experimental.pallas import tpu as pltpu
from jax.sharding import PartitionSpec as P

epsilon = 1e-05
bf16, f32 = jnp.bfloat16, jnp.float32
CHUNK = 128
TILE = 2048
WIDE = 4096
SUB = 256
BLOCK = 32
LAST = 1024
RS1, RS2, RE1, RE2, EC1, EC2, IRS1, IEC1, LRE2, LEC2, LON = range(11)


def dot(a, b):
    return jnp.dot(a, b, preferred_element_type=f32)


def dot_nt(a, b):
    return lax.dot_general(a, b, (((1,), (1,)), ((), ())), preferred_element_type=f32)


def dot_exact(a, b):
    return lax.dot_general(
        a, b, (((1,), (0,)), ((), ())), precision=lax.Precision.HIGHEST, preferred_element_type=f32
    )


def split(x):
    high = x.astype(bf16)
    return high, (x - high.astype(f32)).astype(bf16)


def spread(x, head):
    which = lax.shift_right_logical(lax.broadcasted_iota(jnp.int32, x.shape, 1), 6) + head
    parts = [
        jnp.take_along_axis(x, which + 2 * q, axis=1, mode="promise_in_bounds") for q in range(2)
    ]
    return jnp.concatenate(parts, axis=1)


def collect(halves, gather):
    rows = halves.shape[1]
    total = dot(halves.reshape(2 * rows, SUB), gather)
    return total[:rows] + total[rows:]


def chunks():
    return [(k, slice(k * CHUNK, (k + 1) * CHUNK)) for k in range(2)]


def subs(i, tile=TILE):
    return [
        (
            pl.ds(pl.multiple_of(i * tile + j * SUB, SUB), SUB),
            (tile * i + j * SUB) // 64,
            slice(j * SUB, (j + 1) * SUB),
        )
        for j in range(tile // SUB)
    ]


def each_tile(width, body, tile=TILE):
    def step(i, unused):
        body(i)
        return unused

    lax.fori_loop(0, width // tile, step, 0)


def blocks(k):
    return [
        (slice(r, r + BLOCK), slice(k * CHUNK + r, k * CHUNK + r + BLOCK))
        for r in range(0, CHUNK, BLOCK)
    ]


def params(limit):
    return pltpu.CompilerParams(
        dimension_semantics=("arbitrary",), vmem_limit_bytes=limit * 2**20
    )


def near(shape, dtype=bf16):
    return pltpu.VMEM(shape, dtype)


def kept(shape):
    return pltpu.HBM(shape, bf16)


def on_chip(x):
    return pltpu.with_memory_space_constraint(x, pltpu.VMEM)


def in_hbm(x):
    return pltpu.with_memory_space_constraint(x, pltpu.HBM)


def whole(count):
    return [pl.BlockSpec(memory_space=pltpu.VMEM)] * count


def sending(source, out, sem, i):
    place = pl.ds(pl.multiple_of(i * TILE, TILE), TILE)
    return pltpu.make_async_copy(source.at[:, place], out.at[:, place], sem.at[i])


def loop_params(limit):
    return pltpu.CompilerParams(vmem_limit_bytes=limit * 2**20)


def cost(flops, moved):
    return pl.CostEstimate(flops=int(flops), bytes_accessed=int(moved), transcendentals=0)


def const(shape):
    return pl.BlockSpec(shape, lambda i: (0,) * len(shape))


def decay_kernel(half, on_ref, decay_ref, tok_ref, a_ref, b_ref, row_ref, keep_ref, give_ref, own_ref, other_ref):
    late = on_ref[0]
    turned = tok_ref[...].T
    groups = turned.shape[0] // (2 * half)
    turned = turned.reshape(groups, 2, half, turned.shape[1])
    flat = (groups * half, turned.shape[3])
    lead, trail = turned[:, 0].reshape(flat), turned[:, 1].reshape(flat)
    keep = jnp.where(late > 0.5, trail, lead)
    give = jnp.where(late > 0.5, lead, trail)
    keep_ref[...] = keep
    give_ref[...] = give
    own_ref[...] = keep.T
    other_ref[...] = give.T

    @pl.when(pl.program_id(0) == 0)
    def _():
        n = decay_ref.shape[0]
        lower = lax.broadcasted_iota(jnp.int32, (n, n), 0) >= lax.broadcasted_iota(
            jnp.int32, (n, n), 1
        )
        total = dot_exact(jnp.where(lower, 1.0, 0.0).astype(f32), decay_ref[...])
        middle = [total[k * CHUNK + CHUNK // 2 - 1 :][:1] for k in range(2)]
        end = [total[(k + 1) * CHUNK - 1 :][:1] for k in range(2)]
        for k, rows in chunks():
            a_ref[rows, :] = jnp.exp(total[rows] - middle[k])
            b_ref[rows, :] = jnp.exp(middle[k] - total[rows])
        early = 1.0 - late
        rs1, rs2 = jnp.exp(middle[0]), jnp.exp(middle[1] - end[0])
        re1, re2 = jnp.exp(end[0] - middle[0]), jnp.exp(end[1] - middle[1])
        ec1, ec2 = jnp.exp(end[0]), jnp.exp(end[1] - end[0])
        table = [rs1, rs2, re1, re2, ec1, ec2, rs1 * late, ec1 * late, re2 * early, ec2 * early]
        table.append(jnp.ones_like(rs1) * early)
        table += [jnp.zeros_like(rs1)] * (16 - len(table))
        table = jnp.concatenate(table, axis=0)
        for head in range(0, table.shape[1], SUB // 64):
            row_ref[:, head * 64 : head * 64 + SUB] = spread(table, head)


def decay_call(on, decay, tokens, half, inner):
    n, heads = decay.shape
    width = tokens.shape[1]
    step = max(1024, 2 * half)
    sds = jax.ShapeDtypeStruct
    return pl.pallas_call(
        functools.partial(decay_kernel, half),
        grid=(width // step,),
        in_specs=[
            pl.BlockSpec(memory_space=pltpu.SMEM),
            const((n, heads)),
            pl.BlockSpec((n, step), lambda i: (0, i)),
        ],
        out_specs=[
            const((n, heads)),
            const((n, heads)),
            const((16, inner)),
            pl.BlockSpec((step // 2, n), lambda i: (i, 0)),
            pl.BlockSpec((step // 2, n), lambda i: (i, 0)),
            pl.BlockSpec((n, step // 2), lambda i: (0, i)),
            pl.BlockSpec((n, step // 2), lambda i: (0, i)),
        ],
        out_shape=[
            near((n, heads), f32),
            near((n, heads), f32),
            near((16, inner), f32),
            near((width // 2, n)),
            kept((width // 2, n)),
            near((n, width // 2)),
            near((n, width // 2)),
        ],
        compiler_params=params(24 if half > 512 else 12),
        cost_estimate=cost(1e8, 8e6),
        name="decay",
    )(on, decay, tokens)


def partial_kernel(tok_ref, weight_ref, out_ref):
    part = dot(tok_ref[...], weight_ref[...])

    @pl.when(pl.program_id(0) == 0)
    def _():
        out_ref[...] = part

    @pl.when(pl.program_id(0) > 0)
    def _():
        out_ref[...] += part


def partial_call(tokens, weight):
    n, width = tokens.shape
    cols = weight.shape[1]
    step = 1024
    return pl.pallas_call(
        partial_kernel,
        grid=(width // step,),
        in_specs=[
            pl.BlockSpec((n, step), lambda i: (0, i)),
            pl.BlockSpec((step, cols), lambda i: (i, 0)),
        ],
        out_specs=const((n, cols)),
        out_shape=jax.ShapeDtypeStruct((n, cols), f32),
        compiler_params=params(10),
        cost_estimate=cost(8e8, 4e6),
        name="project_own",
    )(tokens, weight)


def project_kernel(
    tok_ref, weight_ref, part_ref, bias_ref, b_ref,
    lhsy_ref, lhsu_ref, wt_ref, rt_ref, w_ref, r_ref, bs_ref, rho_ref, sc_ref, acc_ref,
):
    i = pl.program_id(0)
    part = dot(tok_ref[...], weight_ref[...])

    @pl.when(i == 0)
    def _():
        acc_ref[...] = part_ref[...] + part

    @pl.when(i > 0)
    def _():
        acc_ref[...] += part

    @pl.when(i == pl.num_programs(0) - 1)
    def _():
        projected = acc_ref[...]
        pre = projected[:, 256:384] + bias_ref[...]
        small = jnp.exp(-jnp.abs(pre))
        step = jnp.maximum(pre, 0.0) + jnp.log1p(small)
        sig = jnp.where(pre >= 0, 1.0, small) / (1.0 + small)
        rho_ref[...] = jnp.where(pre < -15.0, 1.0, sig / jnp.maximum(step, 1e-8))
        bs_ref[...] = step * b_ref[...]
        write = projected[:, :128].astype(bf16)
        read = projected[:, 128:256].astype(bf16)
        w_ref[...] = write
        r_ref[...] = read
        causal = lax.broadcasted_iota(jnp.int32, (CHUNK, CHUNK), 0) >= lax.broadcasted_iota(
            jnp.int32, (CHUNK, CHUNK), 1
        )
        for k, rows in chunks():
            wf, rf = write[rows].astype(f32), read[rows].astype(f32)
            scores = jnp.where(causal, dot_nt(read[rows], write[rows]), 0.0)
            most = jnp.max(jnp.max(jnp.abs(scores), axis=1, keepdims=True), axis=0, keepdims=True)
            power = jnp.exp2(jnp.ceil(jnp.log2(jnp.maximum(most, 1.0))))
            down = 1.0 / power
            lhsy_ref[k] = jnp.concatenate([scores * down, rf * down], axis=1).astype(bf16)
            lhsu_ref[k] = jnp.concatenate([scores.T * down, wf * down], axis=1).astype(bf16)
            wt_ref[k] = wf.T.astype(bf16)
            rt_ref[k] = rf.T.astype(bf16)
            sc_ref[k] = jnp.broadcast_to(power, (8, 128))


def project_call(tokens, weight, part, bias, b):
    n, width = tokens.shape
    cols = weight.shape[1]
    step = 1024
    heads = b.shape[1]
    sds = jax.ShapeDtypeStruct
    shapes = [
        sds((2, CHUNK, 256), bf16),
        sds((2, CHUNK, 256), bf16),
        sds((2, 128, CHUNK), bf16),
        sds((2, 128, CHUNK), bf16),
        sds((n, 128), bf16),
        sds((n, 128), bf16),
        sds((n, heads), f32),
        sds((n, heads), f32),
        sds((2, 8, 128), f32),
    ]
    return pl.pallas_call(
        project_kernel,
        grid=(width // step,),
        in_specs=[
            pl.BlockSpec((n, step), lambda i: (0, i)),
            pl.BlockSpec((step, cols), lambda i: (i, 0)),
            const((n, cols)),
            const((1, heads)),
            const((n, heads)),
        ],
        out_specs=[const(x.shape) for x in shapes],
        out_shape=shapes,
        scratch_shapes=[pltpu.VMEM((n, cols), f32)],
        compiler_params=params(12),
        cost_estimate=cost(8e8, 4e6),
        name="project",
    )(tokens, weight, part, bias, b)


def state_kernel(v_ref, bs_ref, row_ref, wt_ref, x_ref, out_ref, first_ref):
    def tile(i):
        for at, head, _ in subs(i, WIDE):
            rf = row_ref[:, at]
            local = []
            for k, rows in chunks():
                x = (v_ref[rows, at].astype(f32) * spread(bs_ref[rows, :], head)).astype(bf16)
                x_ref[rows, at] = x
                local.append(dot(wt_ref[k], x) * rf[RE1 + k : RE1 + k + 1])
            first_ref[:, at] = local[0].astype(bf16)
            out_ref[:, at] = (rf[EC2 : EC2 + 1] * local[0] + local[1]).astype(bf16)

    each_tile(v_ref.shape[1], tile, WIDE)


def state_call(values, bs, table, wt):
    n, inner = values.shape
    return pl.pallas_call(
        state_kernel,
        in_specs=whole(4),
        out_specs=whole(3),
        out_shape=[near((n, inner)), near((128, inner)), near((128, inner))],
        compiler_params=loop_params(8),
        cost_estimate=cost(2e9, 1.3e7),
        name="states",
    )(on_chip(values), bs, table, wt)


def entering_states(rf, state_ref, first_ref, at):
    state = state_ref[:, at].astype(f32)
    second = rf[IEC1 : IEC1 + 1] * state + first_ref[:, at].astype(f32)
    return (
        (rf[IRS1 : IRS1 + 1] * state).astype(bf16),
        (rf[RS2 : RS2 + 1] * second).astype(bf16),
    )


def outputs_kernel(
    v_ref, o_ref, x_ref, state_ref, first_ref, a_ref, row_ref, lhsy_ref, rt_ref, sc_ref,
    skip_ref, gain_ref,
    out_ref, factors_ref, ga_ref, sgin_ref, sg2_ref,
    pre_ref, square_ref, inner_ref, norm_ref, sem_ref,
):
    channels = v_ref.shape[1]
    steps = channels // TILE
    inv_ref, coef_ref = norm_ref.at[0], norm_ref.at[1]
    square_ref[...] = jnp.zeros_like(square_ref)
    inner_ref[...] = jnp.zeros_like(inner_ref)

    def forward(i):
        for at, head, _ in subs(i):
            entering = entering_states(row_ref[:, at], state_ref, first_ref, at)
            skip, gain = skip_ref[:, at], gain_ref[:, at]
            for k, rows in chunks():
                y = dot(lhsy_ref[k], jnp.concatenate([x_ref[rows, at], entering[k]], axis=0))
                scale = sc_ref[k, 0:1, 0:1]
                for p, r in blocks(k):
                    pre = spread(a_ref[r, :], head) * y[p] * scale
                    pre += skip * v_ref[r, at].astype(f32)
                    pre_ref[r, at] = pre
                    square = pre * pre
                    both = o_ref[r, at].astype(f32) * gain * pre
                    square_ref[r, :] += square[:, :128] + square[:, 128:]
                    inner_ref[r, :] += both[:, :128] + both[:, 128:]
        sending(pre_ref, out_ref, sem_ref, i).start()

    each_tile(channels, forward)
    mean = jnp.sum(square_ref[...], axis=1, keepdims=True) / channels
    inv = lax.rsqrt(mean + epsilon)
    inner = jnp.sum(inner_ref[...], axis=1, keepdims=True) / channels
    inv_ref[...] = jnp.broadcast_to(inv, inv_ref.shape)
    coef_ref[...] = jnp.broadcast_to(inv * inv * inv * inner, coef_ref.shape)
    factors = pltpu.make_async_copy(norm_ref, factors_ref, sem_ref.at[steps])
    factors.start()

    def gradient(i):
        for at, head, _ in subs(i):
            rf = row_ref[:, at]
            gain = gain_ref[:, at]
            grads = []
            for k, rows in chunks():
                for _, r in blocks(k):
                    g = grad_pre(o_ref, pre_ref, inv_ref, coef_ref, gain, r, at)
                    ga_ref[r, at] = (spread(a_ref[r, :], head) * g).astype(bf16)
                grads.append(dot(rt_ref[k], ga_ref[rows, at]) * rf[RS1 + k : RS1 + k + 1])
            sg2_ref[:, at] = grads[1].astype(bf16)
            sgin_ref[:, at] = (grads[0] + rf[EC1 : EC1 + 1] * grads[1]).astype(bf16)

    each_tile(channels, gradient)
    for i in range(steps):
        sending(pre_ref, out_ref, sem_ref, i).wait()
    factors.wait()


def grad_pre(o_ref, pre_ref, inv_ref, coef_ref, gain, r, at):
    inv = jnp.concatenate([inv_ref[r, :]] * 2, axis=1)
    coef = jnp.concatenate([coef_ref[r, :]] * 2, axis=1)
    return inv * (o_ref[r, at].astype(f32) * gain) - pre_ref[r, at] * coef


def outputs_call(
    values, out_grad, x, state, first, a, table, lhsy, rt, sc, skip, gain
):
    n, inner = values.shape
    return pl.pallas_call(
        outputs_kernel,
        in_specs=whole(12),
        out_specs=[pl.BlockSpec(memory_space=pltpu.HBM)] * 2 + whole(3),
        out_shape=[
            pltpu.HBM((n, inner), f32),
            pltpu.HBM((2, n, 128), f32),
            near((n, inner)),
            near((128, inner)),
            near((128, inner)),
        ],
        scratch_shapes=[
            pltpu.VMEM((n, inner), f32),
            pltpu.VMEM((n, 128), f32),
            pltpu.VMEM((n, 128), f32),
            pltpu.VMEM((2, n, 128), f32),
            pltpu.SemaphoreType.DMA((inner // TILE + 1,)),
        ],
        compiler_params=loop_params(16),
        cost_estimate=cost(6e9, 4e7),
        name="outputs",
    )(on_chip(values), on_chip(out_grad), on_chip(x), on_chip(state), on_chip(first), a, table, lhsy, rt, sc, skip, gain)


def read_kernel(ga_ref, x_ref, state_ref, first_ref, row_ref, out_ref):
    out_ref[...] = jnp.zeros_like(out_ref)

    def tile(i):
        sums = [jnp.zeros((CHUNK, 256), f32) for _ in range(2)]
        for at, _, _ in subs(i, WIDE):
            rf = row_ref[:, at]
            entering = entering_states(rf, state_ref, first_ref, at)
            for k, rows in chunks():
                right = jnp.concatenate([x_ref[rows, at], entering[k]], axis=0)
                sums[k] += dot_nt(ga_ref[rows, at], right)
        for k in range(2):
            out_ref[k] += sums[k]

    each_tile(ga_ref.shape[1], tile, WIDE)


def read_call(ga, x, state, first, table):
    return pl.pallas_call(
        read_kernel,
        in_specs=whole(5),
        out_specs=whole(1)[0],
        out_shape=near((2, CHUNK, 256), f32),
        compiler_params=loop_params(8),
        cost_estimate=cost(1.2e9, 1.2e7),
        name="read_grads",
    )(on_chip(ga), on_chip(x), on_chip(state), on_chip(first), table)


def leaving_states(rf, later, sg2_ref, at):
    middle = sg2_ref[:, at].astype(f32) + rf[LEC2 : LEC2 + 1] * later
    return [
        (rf[RE1 : RE1 + 1] * middle).astype(bf16),
        (rf[LRE2 : LRE2 + 1] * later).astype(bf16),
    ]


def backward_kernel(
    ga_ref, x_ref, later_ref, sg2_ref, sout_ref, row_ref, lhsu_ref, sc_ref,
    gather_ref, gsr_ref, w_ref, r_ref, rho_ref,
    gp_ref, sums_ref,
    gw_ref, half_ref,
):
    n = ga_ref.shape[0]
    cols_ref, end_ref = sums_ref.at[:n], sums_ref.at[n:]
    sums_ref[...] = jnp.zeros_like(sums_ref)
    gw_ref[...] = jnp.zeros_like(gw_ref)

    def tile(i):
        sums = jnp.zeros((n + 16, 128), f32)
        writes = jnp.zeros((n, 256), f32)
        for at, _, place in subs(i, WIDE):
            half = half_ref.at[:, :, place]
            rf = row_ref[:, at]
            later = later_ref[:, at].astype(f32)
            leaving = leaving_states(rf, later, sg2_ref, at)
            both = later * sout_ref[:, at].astype(f32) * rf[LON : LON + 1]
            half[0, n:, :], half[1, n:, :] = split(jnp.sum(both.reshape(8, 16, SUB), axis=0))
            for k, rows in chunks():
                u = dot(lhsu_ref[k], jnp.concatenate([ga_ref[rows, at], leaving[k]], axis=0))
                for p, r in blocks(k):
                    half[0, r, :], half[1, r, :] = split(x_ref[r, at].astype(f32) * u[p])
            writes += dot_nt(x_ref[:, at], jnp.concatenate(leaving, axis=0))
            sums += collect(half[...], gather_ref[place, :])
        back = pltpu.roll(sums, WIDE // 64 * i, 1)
        for k, rows in chunks():
            cols_ref[rows, :] += back[rows] * sc_ref[k, 0:1, 0:1]
            gw_ref[rows, :] += writes[rows, 128 * k : 128 * k + 128]
        end_ref[...] += back[n:]

    each_tile(ga_ref.shape[1], tile, WIDE)
    causal = lax.broadcasted_iota(jnp.int32, (CHUNK, CHUNK), 0) >= lax.broadcasted_iota(
        jnp.int32, (CHUNK, CHUNK), 1
    )
    for k, rows in chunks():
        scores = jnp.where(causal, gsr_ref[k, :, :128], 0.0)
        read = gsr_ref[k, :, 128:] + dot(scores.astype(bf16), w_ref[rows, :])
        write = gw_ref[rows, :] + dot(scores.T.astype(bf16), r_ref[rows, :])
        gp_ref[rows, 0:128] = write.astype(bf16)
        gp_ref[rows, 128:256] = read.astype(bf16)
    gp_ref[:, 256:384] = (cols_ref[...] * rho_ref[...]).astype(bf16)


def backward_call(ga, x, later, sg2, sout, table, lhsu, sc, gather, gsr, w, r, rho):
    n, inner = ga.shape
    return pl.pallas_call(
        backward_kernel,
        in_specs=whole(13),
        out_specs=whole(2),
        out_shape=[near((n, 384)), near((n + 16, 128), f32)],
        scratch_shapes=[pltpu.VMEM((n, 128), f32), pltpu.VMEM((2, n + 16, WIDE), bf16)],
        compiler_params=loop_params(14),
        cost_estimate=cost(4e9, 2.5e7),
        name="backward",
    )(on_chip(ga), on_chip(x), on_chip(later), on_chip(sg2), on_chip(sout), table, lhsu, sc, gather, gsr, w, r, rho)


def finish_kernel(
    v_ref, o_ref, pre_ref, ga_ref, later_ref, sg2_ref, row_ref, skip_ref, gain_ref,
    lhsu_ref, bs_ref, a_ref, sc_ref, norm_ref, sums_ref, gather_ref,
    mixed_ref, vg_ref, gd_ref,
    rows_ref, half_ref,
):
    i = pl.program_id(0)
    inv_ref, coef_ref = norm_ref.at[0], norm_ref.at[1]
    sums = jnp.zeros((2 * CHUNK, 128), f32)
    for j in range(LAST // SUB):
        at = slice(j * SUB, (j + 1) * SUB)
        head = (LAST * i + j * SUB) // 64
        leaving = leaving_states(row_ref[:, at], later_ref[:, at].astype(f32), sg2_ref, at)
        skip, gain = skip_ref[:, at], gain_ref[:, at]
        for k, rows in chunks():
            u = dot(lhsu_ref[k], jnp.concatenate([ga_ref[rows, at], leaving[k]], axis=0))
            scale = sc_ref[k, 0:1, 0:1]
            for p, r in blocks(k):
                inv = jnp.concatenate([inv_ref[r, :]] * 2, axis=1)
                mixed_ref[r, at] = (pre_ref[r, at] * inv * gain).astype(bf16)
                g = grad_pre(o_ref, pre_ref, inv_ref, coef_ref, gain, r, at)
                vg = spread(bs_ref[r, :], head) * u[p] * scale + skip * g
                vg_ref[r, at] = vg.astype(bf16)
                mixing = pre_ref[r, at] - skip * v_ref[r, at].astype(f32)
                half_ref[0, r, at], half_ref[1, r, at] = split(ga_ref[r, at].astype(f32) * mixing)
        sums += collect(half_ref[:, :, at], gather_ref[at, :])
    back = pltpu.roll(sums, LAST // 64 * i, 1)

    @pl.when(i == 0)
    def _():
        rows_ref[...] = back

    @pl.when(i > 0)
    def _():
        rows_ref[...] += back

    @pl.when(i == pl.num_programs(0) - 1)
    def _():
        n = o_ref.shape[0]
        upper = lax.broadcasted_iota(jnp.int32, (n, n), 0) <= lax.broadcasted_iota(
            jnp.int32, (n, n), 1
        )
        change = rows_ref[...] / a_ref[...] - sums_ref[:n, :]
        total = dot_exact(jnp.where(upper, 1.0, 0.0).astype(f32), change)
        gd_ref[...] = total + jnp.sum(sums_ref[n:, :], axis=0, keepdims=True)


def finish_call(
    values, out_grad, pre, ga, later, sg2, table, skip, gain, lhsu, bs, a, sc, factors, sums, gather
):
    n, inner = ga.shape

    def tiled(rows):
        return pl.BlockSpec((rows, LAST), lambda i: (0, i))

    return pl.pallas_call(
        finish_kernel,
        grid=(inner // LAST,),
        in_specs=[
            tiled(n),
            tiled(n),
            tiled(n),
            tiled(n),
            tiled(128),
            tiled(128),
            tiled(16),
            tiled(1),
            tiled(1),
            const(lhsu.shape),
            const(bs.shape),
            const(a.shape),
            const(sc.shape),
            const(factors.shape),
            const(sums.shape),
            const((LAST, 128)),
        ],
        out_specs=[tiled(n), tiled(n), const((n, 128))],
        out_shape=[kept((n, inner)), kept((n, inner)), jax.ShapeDtypeStruct((n, 128), f32)],
        scratch_shapes=[pltpu.VMEM((n, 128), f32), pltpu.VMEM((2, n, LAST), bf16)],
        compiler_params=params(15),
        cost_estimate=cost(3e9, 2e7),
        name="finish",
    )(in_hbm(values), in_hbm(out_grad), in_hbm(pre), ga, later, sg2, table, skip, gain, lhsu, bs, a, sc, factors, sums, gather)


def term_kernel(tok_ref, gp_ref, out_ref):
    for start in range(0, tok_ref.shape[0], 256):
        at = slice(start, start + 256)
        out_ref[at, :] = dot(tok_ref[at, :], gp_ref[...])


def term_call(tok, gp):
    return pl.pallas_call(
        term_kernel,
        in_specs=whole(2),
        out_specs=whole(1)[0],
        out_shape=near((tok.shape[0], gp.shape[1]), f32),
        compiler_params=loop_params(4),
        cost_estimate=cost(8e8, 3e6),
        name="term_own",
    )(tok, gp)


def both_kernel(tok_ref, gp_ref, own_ref, out_ref):
    for start in range(0, tok_ref.shape[0], 256):
        at = slice(start, start + 256)
        out_ref[at, :] = (own_ref[at, :] + dot(tok_ref[at, :], gp_ref[...])).astype(bf16)


def both_call(tok, gp, own):
    return pl.pallas_call(
        both_kernel,
        in_specs=whole(3),
        out_specs=whole(1)[0],
        out_shape=jax.ShapeDtypeStruct(own.shape, bf16),
        compiler_params=loop_params(8),
        cost_estimate=cost(8e8, 3e6),
        name="term_both",
    )(on_chip(tok), gp, own)


def total_kernel(parts_ref, out_ref):
    sums = [parts_ref[k].astype(f32) for k in range(parts_ref.shape[0])]
    while len(sums) > 1:
        sums = [sum(sums[k : k + 2]) for k in range(0, len(sums), 2)]
    out_ref[...] = sums[0]


def total_call(parts):
    return pl.pallas_call(
        total_kernel,
        in_specs=whole(1),
        out_specs=whole(1)[0],
        out_shape=near(parts.shape[1:], f32),
        compiler_params=loop_params(4),
        name="total",
    )(on_chip(parts))


SWAP = [(0, 1), (1, 0)]


def on_device(tokens, values, log_decay, out_grad, proj_weight, dt_bias, skip, gain):
    tokens, values, log_decay, out_grad = tokens[0], values[0], log_decay[0], out_grad[0]
    me = lax.axis_index("ctx")
    owners = lax.axis_size("dp")
    n, inner = values.shape
    heads = log_decay.shape[1]
    half = proj_weight.shape[0] // 2
    cols = proj_weight.shape[1]

    mine = lax.dynamic_slice_in_dim(proj_weight, me * half, half, 0)
    own = lax.all_to_all(
        jnp.broadcast_to(mine[None], (owners, half, cols)), "dp", 0, 0, tiled=True
    ).reshape(owners * half, cols)

    late = me.astype(f32).reshape(1)
    a, b, table, keep, give, tok_own, tok_other = decay_call(
        late, log_decay, tokens, half, inner
    )
    lane_head = jnp.arange(WIDE) // (inner // heads)
    gather = (lane_head[:, None] == jnp.arange(128)[None, :]).astype(bf16)
    skip_row = jnp.repeat(skip, inner // heads)[None]
    own, a, b, table, keep, give, gather, skip_row = lax.optimization_barrier(
        (own, a, b, table, keep, give, gather, skip_row)
    )
    other = lax.ppermute(own, "ctx", SWAP)
    part = partial_call(tok_own, own)
    lhsy, lhsu, wt, rt, w, r, bs, rho, sc = project_call(tok_other, other, part, dt_bias[None], b)
    x, sout, first = state_call(values, bs, table, wt)
    state = lax.ppermute(sout, "ctx", SWAP)
    got = lax.ppermute(give, "ctx", SWAP)
    pre, factors, ga, sgin, sg2 = outputs_call(
        values, out_grad, x, state, first, a, table, lhsy, rt, sc, skip_row, gain[None]
    )
    later = lax.ppermute(sgin, "ctx", SWAP)
    gsr = read_call(ga, x, state, first, table)
    gp, sums = backward_call(
        ga, x, later, sg2, sout, table, lhsu, sc, gather, gsr, w, r, rho
    )
    gp_other = lax.ppermute(gp, "ctx", SWAP)
    term = both_call(got, gp_other, term_call(keep, gp))
    parts = lax.all_to_all(term.reshape(owners, half, cols), "dp", 0, 0, tiled=True)
    mixed, grad_values, grad_decay = finish_call(
        values, out_grad, pre, ga, later, sg2, table, skip_row, gain[None], lhsu, bs, a, sc, factors,
        sums, gather[:LAST],
    )
    lead = jnp.where(me == 0, own, other).reshape(owners, half, cols)
    trail = jnp.where(me == 0, other, own).reshape(owners, half, cols)
    weight = jnp.concatenate([lead, trail], axis=1).reshape(2 * owners * half, cols)
    grad_tokens = dot_nt(gp, weight).astype(bf16)
    parts, grad_tokens, mixed, grad_values, grad_decay = lax.optimization_barrier(
        (parts, grad_tokens, mixed, grad_values, grad_decay)
    )
    owned = total_call(parts)
    owned_other = lax.ppermute(owned, "ctx", SWAP)
    grad_weight = jnp.where(
        me == 0,
        jnp.concatenate([owned, owned_other], axis=0),
        jnp.concatenate([owned_other, owned], axis=0),
    )
    return mixed[None], grad_tokens[None], grad_values[None], grad_decay[None], grad_weight


def solution(mesh):
    rows = P("dp", "ctx", None)
    return jax.shard_map(
        on_device,
        mesh=mesh,
        in_specs=(rows, rows, rows, rows, P("dp", None), P(), P(), P()),
        out_specs=(rows, rows, rows, rows, P("dp", None)),
        check_vma=False,
    )
```
